128 devices in a mesh: span: 16 (over z, y_lo, core), wall: 8 (over y_hi, x).
Axes of the slice: x: 4, y: 4 (y_hi: 2, y_lo: 2; y = y_hi * 2 + y_lo), z: 4, core: 2. Of those that a mesh axis runs over, the one named last changes fastest.
Arguments:
- noise: bfloat16 [3, 32, 512, 2048], P(None, None, 'wall', 'span'), may hold values from -6 to 6
- wall_scale: float32 [3], replicated, may hold values from 4 to 12
- span_scale: float32 [3], replicated, may hold values from 4 to 12
- lund_factor: float32 [6, 512], P(None, 'wall'), may hold values from 0.2 to 1
- mean_velocity: float32 [512], P('wall'), may hold values from 0.2 to 1
- owner_map: int32 [8, 16, 512, 1], P('wall', 'span'), may hold values from 0 to 127; in each aligned block of 512 rows (0 to 511, 512 to 1023, ..., all dimensions but the last counted through in order) at most 8 rows name the same one
Outputs:
- face_state: bfloat16 [128, 1024, 1536], P(('span', 'wall'))
The draws below stay inside these ranges and needn't reach their ends.
Inputs may be any that keep to these rules, and one draw needn't show every extreme that they name: `owner_map`: within one tile no owner receives more than 8 elements, and in every draw some tile sends exactly 8 elements to some owner; every device owns some element.
All inputs are finite; a program needn't handle non-finite values.
Results may differ from the reference program's by a relative error of at most 0.001.
Values may be sent and summed in bfloat16 or wider, within the bound.
A program may use at most 64 MiB of HBM per device.

```python
import math
import jax
import jax.numpy as jnp
import numpy as np
from jax import lax

CY = 64
CZ = 128
TPL = 32
HALO = 24
EDGE = 4
NY = 512
NZ = 2048
ELEM_DEV = 512
CAP = 8
PAY = 1536
N_SPAN = 16
N_WALL = 8
DEVICES = 128


def filter_lengths(key, salt):
    base = jax.random.fold_in(key, salt)
    order = jax.random.permutation(jax.random.fold_in(base, 1), 3)
    frac = jax.random.uniform(jax.random.fold_in(base, 2), (3,), jnp.float32)
    return 4.0 * jnp.exp(math.log(3.0) * (order.astype(jnp.float32) + frac) / 3.0)


def draw_wall_scale(key, part):
    return filter_lengths(key, 7001)


def draw_span_scale(key, part):
    return filter_lengths(key, 7002)


def levels(own_key, shape, split, low, top_value):
    gain = 1.0
    for axis_at, blocks in split:
        steps = jax.random.uniform(jax.random.fold_in(jax.random.fold_in(own_key, 6), axis_at), (blocks,), jnp.float32, low / len(split), top_value / len(split))
        gain = gain * jnp.repeat(jnp.exp(steps), shape[axis_at] // blocks).reshape((-1,) + (1,) * (len(shape) - 1 - axis_at))
    return gain


def shared_out(key, own, number, rows, amount, top, most, skew):
    sequence = jax.random.permutation(key, amount)
    heavy_load, usual = load_shares(amount, rows * top, most, skew, True), load_shares(amount, rows * top, most, skew, False)
    places = jnp.arange(amount)

    def named(lengths, turn):
        used = int((lengths > 0).sum())
        fixed = max(1, used // 4)
        passed = fixed + (places - fixed + turn * (used - fixed)) % max(1, amount - fixed)
        return jnp.zeros((amount,), jnp.int32).at[sequence[jnp.where(places < fixed, places, passed)]].set(jnp.asarray(lengths, jnp.int32))

    lengths = jnp.where(number % 4 == 0, named(heavy_load, number // 4), named(usual, number - number // 4 - 1))
    mixed = jax.random.permutation(jax.random.fold_in(own, 3), amount)
    source_of, taker = mixed[0:amount // 2 * 2:2], mixed[1:amount // 2 * 2:2]
    slack = jnp.minimum(lengths[source_of] - 1, most - lengths[taker]) // 2
    slack = jnp.where((source_of == sequence[0]) | (taker == sequence[0]) | (lengths[taker] == 0), 0, jnp.maximum(slack, 0))
    passed = jax.random.randint(jax.random.fold_in(own, 4), (amount // 2,), 0, 1 << 20) % (slack + 1)
    lengths = lengths.at[source_of].add(-passed).at[taker].add(passed)
    items = jnp.searchsorted(jnp.cumsum(lengths), jnp.arange(rows * top), side="right").astype(jnp.int32)
    table = items.reshape(top, rows).T
    table = table[jax.random.permutation(jax.random.fold_in(own, 1), rows)]
    turn = jax.random.randint(jax.random.fold_in(own, 2), (rows, 1), 0, top)
    return jnp.take_along_axis(table, (jnp.arange(top)[None, :] + turn) % top, axis=1)


def load_shares(amount, total, bound, lean, full):
    weights = [(1 << 20) // math.isqrt(grade ** lean) + 1 for grade in range(1, amount + 1)]
    largest = bound if full else min(bound, max(-(-total // amount), total * weights[0] // sum(weights)))
    least = 1 if total - largest >= amount - 1 else 0
    counts, spare = [largest] + [least] * (amount - 1), total - largest - least * (amount - 1)
    while spare > 0:
        free = [i for i in range(1, amount) if counts[i] < largest] or [i for i in range(1, amount) if counts[i] < bound]
        whole, left = sum([weights[i] for i in free]), spare
        for i in free:
            more = min(bound - counts[i], max(1, left * weights[i] // whole), spare)
            counts[i] = counts[i] + more
            spare = spare - more
    return np.array(counts)


def centred(own_key, extent, width, bound, cuts=(), held_as=jnp.bfloat16):
    drawn = jax.random.normal(own_key, extent, jnp.float32) * width
    if len(cuts) > 0:
        drawn = levels(own_key, extent, cuts, -0.22, 0.18) * drawn
    return jnp.clip(drawn, min=-bound, max=bound).astype(held_as)


def setup_inputs(seed: int = 0) -> dict:
    keys = jax.random.split(jax.random.key(seed), 7)
    noise = centred(keys[0], (3, TPL, NY, NZ), 1.0, 6.0, ((2, 8), (3, 16)))
    wall_scale = draw_wall_scale(jax.random.fold_in(keys[6], 71), 0)
    span_scale = draw_span_scale(jax.random.fold_in(keys[6], 71), 0)
    lund_factor = jnp.clip(0.2 + 0.8 * jax.random.uniform(keys[3], (6, NY), jnp.float32) ** levels(keys[3], (6, NY), ((1, 8),), -0.2, 0.2), 0.2, 1.0)
    mean_velocity = jnp.clip(0.2 + 0.8 * jax.random.uniform(keys[4], (NY,), jnp.float32) ** levels(keys[4], (NY,), ((0, 8),), -0.2, 0.2), 0.2, 1.0)
    owner_map_keys = jax.random.split(jax.random.fold_in(keys[5], 1), N_WALL * N_SPAN * ELEM_DEV // ELEM_DEV)
    owner_map_turns = jax.random.permutation(jax.random.fold_in(keys[5], 3), N_WALL * N_SPAN * ELEM_DEV // ELEM_DEV)
    owner_map = jax.vmap(lambda own, number: shared_out(jax.random.fold_in(keys[5], 2), own, number, ELEM_DEV, DEVICES, 1, CAP, 2))(owner_map_keys, owner_map_turns).reshape((N_WALL, N_SPAN, ELEM_DEV, 1))
    return dict(noise=noise, wall_scale=wall_scale, span_scale=span_scale, lund_factor=lund_factor, mean_velocity=mean_velocity, owner_map=owner_map)


def klein_taps(scale):
    offsets = jnp.arange(-HALO, HALO + 1).astype(jnp.float32)
    raw = jnp.exp(-math.pi * offsets * offsets / (2.0 * scale[:, None] * scale[:, None]))
    return raw / jnp.sqrt(lax.optimization_barrier(jnp.sum(raw * raw, axis=1, keepdims=True)))

def filter_plane(packed):
    plane, wall_row, span_row = packed
    padded = jnp.pad(plane, ((HALO, HALO), (0, 0)))
    smooth = jnp.zeros_like(plane)
    for k in range(2 * HALO + 1):
        smooth = smooth + wall_row[k] * padded[k:k + NY]
    result = jnp.zeros_like(plane)
    for k in range(2 * HALO + 1):
        result = result + span_row[k] * jnp.roll(smooth, -(k - HALO), axis=1)
    return result

def reference(noise, wall_scale, span_scale, lund_factor, mean_velocity, owner_map):
    wall_taps = jnp.repeat(klein_taps(wall_scale), TPL, axis=0)
    span_taps = jnp.repeat(klein_taps(span_scale), TPL, axis=0)
    planes = noise.astype(jnp.float32).reshape(3 * TPL, NY, NZ)
    psi = lax.map(filter_plane, (planes, wall_taps, span_taps)).reshape(3, TPL, NY, NZ)
    fac = lund_factor[:, None, :, None]
    along = mean_velocity[None, :, None] + fac[0] * psi[0]
    normal = fac[1] * psi[0] + fac[2] * psi[1]
    spanwise = fac[3] * psi[0] + fac[4] * psi[1] + fac[5] * psi[2]
    velocity = jnp.stack([along, normal, spanwise]).astype(jnp.bfloat16)
    n_wall = NY // CY
    n_span = NZ // CZ
    devices = n_wall * n_span
    cells = velocity.reshape(3, TPL, n_wall, CY // EDGE, EDGE, n_span, CZ // EDGE, EDGE)
    cells = jnp.transpose(cells, (2, 5, 3, 6, 0, 1, 4, 7)).reshape(n_wall, n_span, ELEM_DEV, PAY)
    owners = owner_map[..., 0]
    onehot = (owners[..., None] == jnp.arange(devices, dtype=jnp.int32)).astype(jnp.int32)
    rank = lax.optimization_barrier(jnp.sum(onehot * (jnp.cumsum(onehot, axis=2) - 1), axis=3))
    source = jnp.arange(n_span, dtype=jnp.int32)[None, :] * n_wall + jnp.arange(n_wall, dtype=jnp.int32)[:, None]
    target = owners * (devices * CAP) + source[:, :, None] * CAP + rank
    flat = jnp.zeros((devices * devices * CAP, PAY), jnp.bfloat16)
    flat = flat.at[target.reshape(-1)].set(cells.reshape(-1, PAY))
    return flat.reshape(devices, devices * CAP, PAY)
```

```python
import functools
import math

import jax
import jax.numpy as jnp
from jax import lax
from jax.experimental import pallas as pl
from jax.experimental.pallas import tpu as pltpu
from jax.sharding import PartitionSpec as P

HALO = 24
EDGE = 4
F32 = jnp.float32
BF16 = jnp.bfloat16


def iota(shape, dim):
    return lax.broadcasted_iota(jnp.int32, shape, dim)


def split(x):
    hi = x.astype(BF16)
    return hi, (x - hi.astype(F32)).astype(BF16)


def dot(a, b):
    return jnp.dot(a, b, preferred_element_type=F32)


def dot_nt(a, b):
    return lax.dot_general(a, b, (((1,), (1,)), ((), ())), preferred_element_type=F32)


def tap_coefficients(scale):
    square = jnp.full((1, 128), scale, F32)
    square = square * square
    lane = iota((1, 128), 1)
    k = (lane - HALO).astype(F32)
    energy = jnp.where(lane <= 2 * HALO, jnp.exp(-math.pi * k * k / square), 0.0)
    norm = jnp.sqrt(jnp.sum(energy, axis=1, keepdims=True))
    return (math.pi / (2.0 * square))[:, :1], 1.0 / norm


def tap_values(offset, valid, coefficients):
    rate, gain = coefficients
    d = offset.astype(F32)
    inside = valid & (offset >= -HALO) & (offset <= HALO)
    return jnp.where(inside, jnp.exp(-(d * d) * rate) * gain, 0.0)


def wall_operand(scale, wall, n_wall):
    shape = (128, 224)
    r, k = iota(shape, 0), iota(shape, 1)
    y = EDGE * (r >> 3) + (r & 3)
    t = (r >> 2) & 1
    core, low = k < 128, k < 176
    j = jnp.where(low, k - 128, k - 176)
    t_halo = (j >= HALO).astype(jnp.int32)
    inner = j - HALO * t_halo
    t_col = jnp.where(core, k >> 6, t_halo)
    y_col = jnp.where(core, k & 63, jnp.where(low, inner - HALO, inner + 64))
    first = (wall > 0).astype(jnp.int32)
    last = (wall < n_wall - 1).astype(jnp.int32)
    present = jnp.where(core, 1, jnp.where(low, first, last)) > 0
    values = tap_values(y_col - y, (t == t_col) & present, tap_coefficients(scale))
    hi, lo = split(values)
    return jnp.concatenate([hi, lo], axis=0)


def span_operands(scale):
    coefficients = tap_coefficients(scale)
    shape = (128, 128)
    r, k = iota(shape, 0), iota(shape, 1)
    z = EDGE * (r & 31) + (r >> 5)
    hi, lo = split(tap_values(k - z, r >= 0, coefficients))
    row, col = iota((96, 256), 0), iota((96, 256), 1)
    g = (row >= 24).astype(jnp.int32) + (row >= 48).astype(jnp.int32) + (row >= 72).astype(jnp.int32)
    inner = row - HALO * g
    source = inner + jnp.where(g < 2, 128 - HALO, 0) + 128 * (g & 1)
    pick = jnp.where(col == source, 1.0, 0.0).astype(BF16)
    own = jnp.concatenate(
        [
            jnp.concatenate([hi, hi], axis=1),
            jnp.concatenate([lo, jnp.zeros_like(lo)], axis=1),
            pick,
        ],
        axis=0,
    )
    shape = (128, 192)
    r, k = iota(shape, 0), iota(shape, 1)
    z = EDGE * (r & 31) + (r >> 5)
    second = k >= 96
    j = jnp.where(second, k - 96, k)
    right = j >= 48
    j = jnp.where(right, j - 48, j)
    low_term = j >= HALO
    j = jnp.where(low_term, j - HALO, j)
    column = jnp.where(right, 128 + j, j - HALO)
    values = tap_values(column - z, r >= 0, coefficients)
    hi = values.astype(BF16).astype(F32)
    strips = jnp.where(second, jnp.where(low_term, 0.0, values - hi), hi).astype(BF16)
    return own, strips


def wall_pass(c, noise_ref, low_ref, high_ref, operand, smooth_ref):
    planes = noise_ref.shape[1]
    for q in range(planes // 4):
        blocks = []
        for p in (2 * q, 2 * q + 1):
            at = (c * planes // 2 + p) * 2 * HALO
            blocks.append(
                jnp.concatenate(
                    [
                        noise_ref[c, 2 * p : 2 * p + 2].reshape(128, 128),
                        low_ref[at : at + 2 * HALO],
                        high_ref[at : at + 2 * HALO],
                    ],
                    axis=0,
                )
            )
        both = dot(operand, jnp.concatenate(blocks, axis=1))
        both = both[:128] + both[128:]
        smooth_ref[:, 2 * q] = both[:, :128].reshape(16, 8, 128)
        smooth_ref[:, 2 * q + 1] = both[:, 128:].reshape(16, 8, 128)


def front_kernel(n_wall, wscale, sscale, noise_ref, low_ref, high_ref, centre_ref, to_next_ref, to_prev_ref, smooth_ref):
    wall = lax.axis_index("wall")
    for c in range(3):
        wall_pass(c, noise_ref, low_ref, high_ref, wall_operand(wscale[c], wall, n_wall), smooth_ref)
        own, _ = span_operands(sscale[c])
        for g in range(8):
            hi, lo = split(smooth_ref[2 * g : 2 * g + 2].reshape(256, 128))
            out = dot_nt(own, jnp.concatenate([hi, lo], axis=1))
            lanes = slice(256 * g, 256 * g + 256)
            centre_ref[c, :, lanes] = out[:128] + out[128:256]
            to_next_ref[c, :, lanes] = out[256:304].astype(BF16)
            to_prev_ref[c, :, lanes] = out[304:352].astype(BF16)


def lane_factors(fac):
    first, rest = fac.astype(BF16), None
    rest = fac - first.astype(F32)
    second = rest.astype(BF16)
    third = (rest - second.astype(F32)).astype(BF16)
    lane = iota((64, 2048), 1)
    spread = jnp.where(iota((64, 2048), 0) == EDGE * (lane >> 7) + (lane & 3), 1.0, 0.0).astype(BF16)
    return dot(first, spread) + dot(second, spread) + dot(third, spread)


def slot_onehot(owner, devices, slots):
    n = owner.shape[1]
    mine = jnp.where(iota((devices, n), 0) == owner, 1.0, 0.0)
    before = jnp.where(iota((n, n), 0) < iota((n, n), 1), 1.0, 0.0).astype(BF16)
    count = dot(mine.astype(BF16), before)
    rank = jnp.sum(mine * count, axis=0, keepdims=True).astype(jnp.int32)
    target = owner * slots + rank
    return jnp.where(iota((devices * slots, n), 0) == target, 1.0, 0.0).astype(BF16)


def interleave_matrix():
    k, n = iota((512, 512), 0), iota((512, 512), 1)
    return jnp.where(n == EDGE * (k & 127) + (k >> 7), 1.0, 0.0).astype(BF16)


def velocity_of(c, psi, fac_ref, lanes):
    def f(i):
        return fac_ref[i : i + 1, lanes]

    if c == 0:
        return f(6) + f(0) * psi[0]
    if c == 1:
        return f(1) * psi[0] + f(2) * psi[1]
    return f(3) * psi[0] + f(4) * psi[1] + f(5) * psi[2]


def back_kernel(devices, slots, sscale, centre_ref, left_ref, right_ref, fac_ref, owner_ref, out_ref, psi_ref, lanes_ref, hot_ref, tile_ref):
    lanes_ref[...] = lane_factors(fac_ref[...])
    hot_ref[...] = slot_onehot(owner_ref[...], devices, slots)
    interleave = interleave_matrix()
    for c in range(3):
        _, strips = span_operands(sscale[c])
        for g in range(8):
            lanes = slice(256 * g, 256 * g + 256)
            left, right = left_ref[c, :, lanes], right_ref[c, :, lanes]
            psi_c = centre_ref[c, :, lanes] + dot(strips, jnp.concatenate([left, right, left, right], axis=0))
            if c < 2:
                psi_ref[c, :, lanes] = psi_c
            psi = [psi_ref[i, :, lanes] for i in range(c)] + [psi_c]
            velocity = velocity_of(c, psi, lanes_ref, lanes).astype(BF16)
            for e in range(2):
                for dz in range(EDGE):
                    tile_ref[32 * (2 * g + e) : 32 * (2 * g + e) + 32, 128 * dz : 128 * dz + 128] = velocity[
                        32 * dz : 32 * dz + 32, 128 * e : 128 * e + 128
                    ]
        payload = dot(tile_ref[...], interleave).astype(BF16)
        for b in range(4):
            rows = slice(256 * b, 256 * b + 256)
            out_ref[rows, 512 * c : 512 * c + 512] = dot(hot_ref[rows], payload).astype(BF16)


VMEM = pl.BlockSpec(memory_space=pltpu.VMEM)
SMEM = pl.BlockSpec(memory_space=pltpu.SMEM)


def front(noise, low, high, wall_scale, span_scale, n_wall):
    return pl.pallas_call(
        functools.partial(front_kernel, n_wall),
        out_shape=(
            jax.ShapeDtypeStruct((3, 128, 2048), F32),
            jax.ShapeDtypeStruct((3, 48, 2048), BF16),
            jax.ShapeDtypeStruct((3, 48, 2048), BF16),
        ),
        in_specs=[SMEM, SMEM, VMEM, VMEM, VMEM],
        out_specs=(VMEM, VMEM, VMEM),
        scratch_shapes=[pltpu.VMEM((16, 16, 8, 128), F32)],
        name="front",
    )(wall_scale, span_scale, noise, low, high)


def back(centre, left, right, fac, owner, span_scale, devices, slots):
    return pl.pallas_call(
        functools.partial(back_kernel, devices, slots),
        out_shape=jax.ShapeDtypeStruct((devices * slots, 1536), BF16),
        in_specs=[SMEM, VMEM, VMEM, VMEM, VMEM, VMEM],
        out_specs=VMEM,
        scratch_shapes=[
            pltpu.VMEM((2, 128, 2048), F32),
            pltpu.VMEM((8, 2048), F32),
            pltpu.VMEM((devices * slots, 512), BF16),
            pltpu.VMEM((512, 512), BF16),
        ],
        name="back",
    )(span_scale, centre, left, right, fac, owner)


def per_device(noise, wall_scale, span_scale, lund_factor, mean_velocity, owner_map):
    planes, rows = noise.shape[1:3]
    n_span, n_wall = lax.axis_size("span"), lax.axis_size("wall")
    devices = n_span * n_wall
    slots = 8
    up = [(i, (i + 1) % n_wall) for i in range(n_wall)]
    down = [(b, a) for a, b in up]
    low = lax.ppermute(noise[:, :, rows - HALO :], "wall", up)
    high = lax.ppermute(noise[:, :, :HALO], "wall", down)
    fac = jnp.concatenate([lund_factor, mean_velocity[None], jnp.zeros((1, rows), F32)], axis=0)
    centre, to_next, to_prev = front(
        noise, low.reshape(-1, 128), high.reshape(-1, 128), wall_scale, span_scale, n_wall
    )
    ahead = [(i, (i + 1) % n_span) for i in range(n_span)]
    left = lax.ppermute(to_next, "span", ahead)
    right = lax.ppermute(to_prev, "span", [(b, a) for a, b in ahead])
    outgoing = back(centre, left, right, fac, owner_map.reshape(1, -1), span_scale, devices, slots)
    received = lax.all_to_all(
        outgoing.reshape(devices, slots, -1), ("span", "wall"), split_axis=0, concat_axis=0, tiled=True
    )
    return received.reshape(1, devices * slots, -1)


def solution(mesh):
    return jax.shard_map(
        per_device,
        mesh=mesh,
        in_specs=(
            P(None, None, "wall", "span"),
            P(),
            P(),
            P(None, "wall"),
            P("wall"),
            P("wall", "span", None, None),
        ),
        out_specs=P(("span", "wall"), None, None),
        check_vma=False,
    )
```

```python
import functools
import math

import jax
import jax.numpy as jnp
from jax import lax
from jax.experimental import pallas as pl
from jax.experimental.pallas import tpu as pltpu
from jax.sharding import PartitionSpec as P

HALO = 24
EDGE = 4
F32 = jnp.float32
BF16 = jnp.bfloat16


def iota(shape, dim):
    return lax.broadcasted_iota(jnp.int32, shape, dim)


def split(x):
    hi = x.astype(BF16)
    return hi, (x - hi.astype(F32)).astype(BF16)


def dot(a, b):
    return jnp.dot(a, b, preferred_element_type=F32)


def dot_nt(a, b):
    return lax.dot_general(a, b, (((1,), (1,)), ((), ())), preferred_element_type=F32)


def tap_coefficients(scale):
    square = jnp.full((1, 128), scale, F32)
    square = square * square
    lane = iota((1, 128), 1)
    k = (lane - HALO).astype(F32)
    energy = jnp.where(lane <= 2 * HALO, jnp.exp(-math.pi * k * k / square), 0.0)
    norm = jnp.sqrt(jnp.sum(energy, axis=1, keepdims=True))
    return (math.pi / (2.0 * square))[:, :1], 1.0 / norm


def tap_values(offset, valid, coefficients):
    rate, gain = coefficients
    d = offset.astype(F32)
    inside = valid & (offset >= -HALO) & (offset <= HALO)
    return jnp.where(inside, jnp.exp(-(d * d) * rate) * gain, 0.0)


def wall_operand(scale, wall, n_wall):
    shape = (128, 224)
    r, k = iota(shape, 0), iota(shape, 1)
    y = EDGE * (r >> 3) + (r & 3)
    t = (r >> 2) & 1
    core, low = k < 128, k < 176
    j = jnp.where(low, k - 128, k - 176)
    t_halo = (j >= HALO).astype(jnp.int32)
    inner = j - HALO * t_halo
    t_col = jnp.where(core, k >> 6, t_halo)
    y_col = jnp.where(core, k & 63, jnp.where(low, inner - HALO, inner + 64))
    first = (wall > 0).astype(jnp.int32)
    last = (wall < n_wall - 1).astype(jnp.int32)
    present = jnp.where(core, 1, jnp.where(low, first, last)) > 0
    values = tap_values(y_col - y, (t == t_col) & present, tap_coefficients(scale))
    hi, lo = split(values)
    return jnp.concatenate([hi, lo], axis=0)


def span_operands(scale):
    coefficients = tap_coefficients(scale)
    shape = (128, 128)
    r, k = iota(shape, 0), iota(shape, 1)
    z = EDGE * (r & 31) + (r >> 5)
    hi, lo = split(tap_values(k - z, r >= 0, coefficients))
    row, col = iota((96, 256), 0), iota((96, 256), 1)
    g = (row >= 24).astype(jnp.int32) + (row >= 48).astype(jnp.int32) + (row >= 72).astype(jnp.int32)
    inner = row - HALO * g
    source = inner + jnp.where(g < 2, 128 - HALO, 0) + 128 * (g & 1)
    pick = jnp.where(col == source, 1.0, 0.0).astype(BF16)
    own = jnp.concatenate(
        [
            jnp.concatenate([hi, hi], axis=1),
            jnp.concatenate([lo, jnp.zeros_like(lo)], axis=1),
            pick,
        ],
        axis=0,
    )
    shape = (128, 192)
    r, k = iota(shape, 0), iota(shape, 1)
    z = EDGE * (r & 31) + (r >> 5)
    second = k >= 96
    j = jnp.where(second, k - 96, k)
    right = j >= 48
    j = jnp.where(right, j - 48, j)
    low_term = j >= HALO
    j = jnp.where(low_term, j - HALO, j)
    column = jnp.where(right, 128 + j, j - HALO)
    values = tap_values(column - z, r >= 0, coefficients)
    hi = values.astype(BF16).astype(F32)
    strips = jnp.where(second, jnp.where(low_term, 0.0, values - hi), hi).astype(BF16)
    return own, strips


def wall_pass(c, noise_ref, low_ref, high_ref, operand, smooth_ref):
    planes = noise_ref.shape[1]
    for q in range(planes // 4):
        blocks = []
        for p in (2 * q, 2 * q + 1):
            blocks.append(
                jnp.concatenate(
                    [
                        noise_ref[c, 2 * p : 2 * p + 2].reshape(128, 128),
                        low_ref[c, 2 * p : 2 * p + 2].reshape(2 * HALO, 128),
                        high_ref[c, 2 * p : 2 * p + 2].reshape(2 * HALO, 128),
                    ],
                    axis=0,
                )
            )
        both = dot(operand, jnp.concatenate(blocks, axis=1))
        both = both[:128] + both[128:]
        smooth_ref[:, 2 * q] = both[:, :128].reshape(16, 8, 128)
        smooth_ref[:, 2 * q + 1] = both[:, 128:].reshape(16, 8, 128)


def span_own_pass(c, own, smooth_ref, psi_ref, to_next_ref, to_prev_ref):
    for g in range(8):
        hi, lo = split(smooth_ref[2 * g : 2 * g + 2].reshape(256, 128))
        out = dot_nt(own, jnp.concatenate([hi, lo], axis=1))
        lanes = slice(256 * g, 256 * g + 256)
        psi_ref[c, :, lanes] = out[:128] + out[128:256]
        to_next_ref[c, :, lanes] = out[256:304].astype(BF16)
        to_prev_ref[c, :, lanes] = out[304:352].astype(BF16)


def lane_factors(fac):
    first, rest = fac.astype(BF16), None
    rest = fac - first.astype(F32)
    second = rest.astype(BF16)
    third = (rest - second.astype(F32)).astype(BF16)
    lane = iota((64, 2048), 1)
    spread = jnp.where(iota((64, 2048), 0) == EDGE * (lane >> 7) + (lane & 3), 1.0, 0.0).astype(BF16)
    return dot(first, spread) + dot(second, spread) + dot(third, spread)


def slot_onehot(owner, devices, slots):
    n = owner.shape[1]
    mine = jnp.where(iota((devices, n), 0) == owner, 1.0, 0.0)
    before = jnp.where(iota((n, n), 0) < iota((n, n), 1), 1.0, 0.0).astype(BF16)
    count = dot(mine.astype(BF16), before)
    rank = jnp.sum(mine * count, axis=0, keepdims=True).astype(jnp.int32)
    target = owner * slots + rank
    return jnp.where(iota((devices * slots, n), 0) == target, 1.0, 0.0).astype(BF16)


def interleave_matrix():
    k, n = iota((512, 512), 0), iota((512, 512), 1)
    return jnp.where(n == EDGE * (k & 127) + (k >> 7), 1.0, 0.0).astype(BF16)


def velocity_of(c, psi, fac_ref, lanes):
    def f(i):
        return fac_ref[i : i + 1, lanes]

    if c == 0:
        return f(6) + f(0) * psi[0]
    if c == 1:
        return f(1) * psi[0] + f(2) * psi[1]
    return f(3) * psi[0] + f(4) * psi[1] + f(5) * psi[2]


def finish(c, strips, left_ref, right_ref, psi_ref, lanes_ref, hot_ref, interleave_ref, tile_ref, outgoing_ref):
    for g in range(8):
        lanes = slice(256 * g, 256 * g + 256)
        left, right = left_ref[c, :, lanes], right_ref[c, :, lanes]
        psi_c = psi_ref[c, :, lanes] + dot(strips, jnp.concatenate([left, right, left, right], axis=0))
        if c < 2:
            psi_ref[c, :, lanes] = psi_c
        psi = [psi_ref[i, :, lanes] for i in range(c)] + [psi_c]
        velocity = velocity_of(c, psi, lanes_ref, lanes).astype(BF16)
        for e in range(2):
            for dz in range(EDGE):
                tile_ref[32 * (2 * g + e) : 32 * (2 * g + e) + 32, 128 * dz : 128 * dz + 128] = velocity[
                    32 * dz : 32 * dz + 32, 128 * e : 128 * e + 128
                ]
    payload = dot(tile_ref[...], interleave_ref[...]).astype(BF16)
    for b in range(4):
        part = dot(hot_ref[256 * b : 256 * b + 256], payload)
        outgoing_ref[c, 32 * b : 32 * b + 32] = part.reshape(32, 8, 512).astype(BF16)


def kernel(
    n_span, n_wall, slots, wscale, sscale, noise_hbm, lund_ref, mean_ref, owner_ref, out_ref,
    noise_ref, low_ref, high_ref, smooth_ref, psi_ref, to_next_ref, to_prev_ref, left_ref, right_ref,
    fac_ref, lanes_ref, hot_ref, interleave_ref, tile_ref, outgoing_ref,
    load_sem, halo_send, halo_recv, strip_send, strip_recv, out_send, out_recv, self_sem,
):
    devices = n_span * n_wall
    span, wall = lax.axis_index("span"), lax.axis_index("wall")
    me = span * n_wall + wall
    rows = noise_hbm.shape[2]

    def place(index):
        return {"span": lax.div(index, n_wall), "wall": lax.rem(index, n_wall)}

    barrier = pltpu.get_barrier_semaphore()

    def greet(i, carry):
        pl.semaphore_signal(barrier, inc=1, device_id=place(jnp.bitwise_xor(me, i)), device_id_type=MESH)
        return carry

    lax.fori_loop(1, devices, greet, 0)

    loads = [pltpu.make_async_copy(noise_hbm.at[c], noise_ref.at[c], load_sem.at[c]) for c in range(3)]
    for load in loads:
        load.start()
    fac_ref[...] = jnp.zeros_like(fac_ref)
    fac_ref[0:6] = lund_ref[...]
    fac_ref[6:7] = mean_ref[...]
    lanes_ref[...] = lane_factors(fac_ref[...])
    hot_ref[...] = slot_onehot(owner_ref[...], devices, slots)
    interleave_ref[...] = interleave_matrix()

    def sends(c, step, size, axis, pairs, send_sem, recv_sem):
        here = lax.axis_index(axis)
        targets = (lax.rem(here + 1, size), lax.rem(here + size - 1, size))
        return [
            pltpu.make_async_remote_copy(
                src_ref=src, dst_ref=dst, send_sem=send_sem.at[c, i], recv_sem=recv_sem.at[c, i],
                device_id={axis: targets[i]}, device_id_type=MESH,
            )
            for i, (src, dst) in enumerate(pairs)
        ]

    halos = [
        sends(
            c, 0, n_wall, "wall",
            (
                (noise_hbm.at[c, :, pl.ds(rows - HALO, HALO), :], low_ref.at[c]),
                (noise_hbm.at[c, :, pl.ds(0, HALO), :], high_ref.at[c]),
            ),
            halo_send, halo_recv,
        )
        for c in range(3)
    ]
    strips = [
        sends(
            c, 1, n_span, "span",
            ((to_next_ref.at[c], left_ref.at[c]), (to_prev_ref.at[c], right_ref.at[c])),
            strip_send, strip_recv,
        )
        for c in range(3)
    ]

    pl.semaphore_wait(barrier, devices - 1)
    for c in range(3):
        for copy in halos[c]:
            copy.start()

    def early(c):
        operand = wall_operand(wscale[c], wall, n_wall)
        own, from_strips = span_operands(sscale[c])
        loads[c].wait()
        for copy in halos[c]:
            copy.wait_recv()
        wall_pass(c, noise_ref, low_ref, high_ref, operand, smooth_ref)
        span_own_pass(c, own, smooth_ref, psi_ref, to_next_ref, to_prev_ref)
        for copy in strips[c]:
            copy.start()
        return from_strips

    def late(c, from_strips):
        for copy in strips[c]:
            copy.wait_recv()
        finish(c, from_strips, left_ref, right_ref, psi_ref, lanes_ref, hot_ref, interleave_ref, tile_ref, outgoing_ref)
        lanes = pl.ds(512 * c, 512)

        def deliver(i, carry):
            to = jnp.bitwise_xor(me, i)
            pltpu.make_async_remote_copy(
                src_ref=outgoing_ref.at[c, to], dst_ref=out_ref.at[me, :, lanes],
                send_sem=out_send.at[c], recv_sem=out_recv.at[c], device_id=place(to), device_id_type=MESH,
            ).start()
            return carry

        lax.fori_loop(1, devices, deliver, 0)
        pltpu.make_async_copy(outgoing_ref.at[c, me], out_ref.at[me, :, lanes], self_sem.at[c]).start()

    first = early(0)
    second = early(1)
    late(0, first)
    third = early(2)
    late(1, second)
    late(2, third)

    others = pl.ds(0, devices - 1)
    for c in range(3):
        for copy in halos[c] + strips[c]:
            copy.wait_send()
        lanes = pl.ds(512 * c, 512)
        pltpu.make_async_copy(outgoing_ref.at[c, me], out_ref.at[me, :, lanes], self_sem.at[c]).wait()
        pltpu.make_async_copy(outgoing_ref.at[c, others], outgoing_ref.at[c, others], out_send.at[c]).wait()
        pltpu.make_async_copy(out_ref.at[others, :, lanes], out_ref.at[others, :, lanes], out_recv.at[c]).wait()


VMEM = pl.BlockSpec(memory_space=pltpu.VMEM)
SMEM = pl.BlockSpec(memory_space=pltpu.SMEM)
ANY = pl.BlockSpec(memory_space=pl.ANY)
MESH = pl.DeviceIdType.MESH


def per_device(noise, wall_scale, span_scale, lund_factor, mean_velocity, owner_map):
    n_span, n_wall = lax.axis_size("span"), lax.axis_size("wall")
    devices = n_span * n_wall
    slots = 8
    received = pl.pallas_call(
        functools.partial(kernel, n_span, n_wall, slots),
        out_shape=jax.ShapeDtypeStruct((devices, slots, 1536), BF16),
        in_specs=[SMEM, SMEM, ANY, VMEM, VMEM, VMEM],
        out_specs=ANY,
        scratch_shapes=[
            pltpu.VMEM(noise.shape, BF16),
            pltpu.VMEM((3, 32, HALO, 128), BF16),
            pltpu.VMEM((3, 32, HALO, 128), BF16),
            pltpu.VMEM((16, 16, 8, 128), F32),
            pltpu.VMEM((3, 128, 2048), F32),
            pltpu.VMEM((3, 2 * HALO, 2048), BF16),
            pltpu.VMEM((3, 2 * HALO, 2048), BF16),
            pltpu.VMEM((3, 2 * HALO, 2048), BF16),
            pltpu.VMEM((3, 2 * HALO, 2048), BF16),
            pltpu.VMEM((8, 64), F32),
            pltpu.VMEM((8, 2048), F32),
            pltpu.VMEM((devices * slots, 512), BF16),
            pltpu.VMEM((512, 512), BF16),
            pltpu.VMEM((512, 512), BF16),
            pltpu.VMEM((3, devices, slots, 512), BF16),
            pltpu.SemaphoreType.DMA((3,)),
            pltpu.SemaphoreType.DMA((3, 2)),
            pltpu.SemaphoreType.DMA((3, 2)),
            pltpu.SemaphoreType.DMA((3, 2)),
            pltpu.SemaphoreType.DMA((3, 2)),
            pltpu.SemaphoreType.DMA((3,)),
            pltpu.SemaphoreType.DMA((3,)),
            pltpu.SemaphoreType.DMA((3,)),
        ],
        compiler_params=pltpu.CompilerParams(collective_id=0, has_side_effects=True, vmem_limit_bytes=60 << 20),
        name="inflow",
    )(
        wall_scale, span_scale, noise, lund_factor, mean_velocity.reshape(1, -1), owner_map.reshape(1, -1)
    )
    return received.reshape(1, devices * slots, -1)


def solution(mesh):
    return jax.shard_map(
        per_device,
        mesh=mesh,
        in_specs=(
            P(None, None, "wall", "span"),
            P(),
            P(),
            P(None, "wall"),
            P("wall"),
            P("wall", "span", None, None),
        ),
        out_specs=P(("span", "wall"), None, None),
        check_vma=False,
    )
```

```python
import functools
import math

import jax
import jax.numpy as jnp
from jax import lax
from jax.experimental import pallas as pl
from jax.experimental.pallas import tpu as pltpu
from jax.sharding import PartitionSpec as P

HALO = 24
EDGE = 4
STRIP = 32
F32 = jnp.float32
BF16 = jnp.bfloat16


def iota(shape, dim):
    return lax.broadcasted_iota(jnp.int32, shape, dim)


def split(x):
    hi = x.astype(BF16)
    return hi, (x - hi.astype(F32)).astype(BF16)


def dot(a, b):
    return jnp.dot(a, b, preferred_element_type=F32)


def dot_nt(a, b):
    return lax.dot_general(a, b, (((1,), (1,)), ((), ())), preferred_element_type=F32)


def tap_coefficients(scale):
    square = jnp.full((1, 128), scale, F32)
    square = square * square
    lane = iota((1, 128), 1)
    k = (lane - HALO).astype(F32)
    energy = jnp.where(lane <= 2 * HALO, jnp.exp(-math.pi * k * k / square), 0.0)
    norm = jnp.sqrt(jnp.sum(energy, axis=1, keepdims=True))
    return (math.pi / (2.0 * square))[:, :1], 1.0 / norm


def tap_values(offset, valid, coefficients):
    rate, gain = coefficients
    d = offset.astype(F32)
    inside = valid & (offset >= -HALO) & (offset <= HALO)
    return jnp.where(inside, jnp.exp(-(d * d) * rate) * gain, 0.0)


def wall_operand(scale, wall, n_wall):
    shape = (128, 224)
    r, k = iota(shape, 0), iota(shape, 1)
    y = EDGE * (r >> 3) + (r & 3)
    t = (r >> 2) & 1
    core, low = k < 128, k < 176
    j = jnp.where(low, k - 128, k - 176)
    t_halo = (j >= HALO).astype(jnp.int32)
    inner = j - HALO * t_halo
    t_col = jnp.where(core, k >> 6, t_halo)
    y_col = jnp.where(core, k & 63, jnp.where(low, inner - HALO, inner + 64))
    first = (wall > 0).astype(jnp.int32)
    last = (wall < n_wall - 1).astype(jnp.int32)
    present = jnp.where(core, 1, jnp.where(low, first, last)) > 0
    values = tap_values(y_col - y, (t == t_col) & present, tap_coefficients(scale))
    hi, lo = split(values)
    return jnp.concatenate([hi, lo], axis=0)


def span_operands(scale):
    coefficients = tap_coefficients(scale)
    shape = (128, 128)
    r, k = iota(shape, 0), iota(shape, 1)
    z = EDGE * (r & 31) + (r >> 5)
    hi, lo = split(tap_values(k - z, r >= 0, coefficients))
    row, col = iota((2 * STRIP, 256), 0), iota((2 * STRIP, 256), 1)
    j = row & (STRIP - 1)
    low_term = j >= HALO
    to_next = jnp.where(low_term, 256 - STRIP + j, 128 - HALO + j)
    to_prev = jnp.where(low_term, 128 - HALO + j, j)
    pick = jnp.where(col == jnp.where(row < STRIP, to_next, to_prev), 1.0, 0.0).astype(BF16)
    own = jnp.concatenate(
        [
            jnp.concatenate([hi, hi], axis=1),
            jnp.concatenate([lo, jnp.zeros_like(lo)], axis=1),
            pick,
        ],
        axis=0,
    )
    second = k >= 2 * STRIP
    j = k & (STRIP - 1)
    low_term = j >= HALO
    from_left = jnp.where(low_term, j - STRIP, j - HALO)
    from_right = jnp.where(low_term, 128 + j - HALO, 128 + j)
    column = jnp.where((k & STRIP) > 0, from_right, from_left)
    values = tap_values(column - z, r >= 0, coefficients)
    hi = values.astype(BF16).astype(F32)
    strips = jnp.where(second, jnp.where(low_term, 0.0, values - hi), hi).astype(BF16)
    return own, strips


def wall_pass(c, noise_ref, low_ref, high_ref, operand, smooth_ref):
    planes = noise_ref.shape[1]
    for q in range(planes // 4):
        blocks = []
        for p in (2 * q, 2 * q + 1):
            blocks.append(
                jnp.concatenate(
                    [
                        noise_ref[c, 2 * p : 2 * p + 2].reshape(128, 128),
                        low_ref[c, 2 * p : 2 * p + 2].reshape(2 * HALO, 128),
                        high_ref[c, 2 * p : 2 * p + 2].reshape(2 * HALO, 128),
                    ],
                    axis=0,
                )
            )
        both = dot(operand, jnp.concatenate(blocks, axis=1))
        both = both[:128] + both[128:]
        smooth_ref[:, 2 * q] = both[:, :128].reshape(16, 8, 128)
        smooth_ref[:, 2 * q + 1] = both[:, 128:].reshape(16, 8, 128)


def span_own_pass(c, own, smooth_ref, psi_ref, to_next_ref, to_prev_ref):
    for g in range(8):
        hi, lo = split(smooth_ref[2 * g : 2 * g + 2].reshape(256, 128))
        out = dot_nt(own, jnp.concatenate([hi, lo], axis=1))
        lanes = slice(256 * g, 256 * g + 256)
        psi_ref[c, :, lanes] = out[:128] + out[128:256]
        to_next_ref[c, :, lanes] = out[256 : 256 + STRIP].astype(BF16)
        to_prev_ref[c, :, lanes] = out[256 + STRIP :].astype(BF16)


def lane_factors(fac):
    first, rest = fac.astype(BF16), None
    rest = fac - first.astype(F32)
    second = rest.astype(BF16)
    third = (rest - second.astype(F32)).astype(BF16)
    lane = iota((64, 2048), 1)
    spread = jnp.where(iota((64, 2048), 0) == EDGE * (lane >> 7) + (lane & 3), 1.0, 0.0).astype(BF16)
    return dot(first, spread) + dot(second, spread) + dot(third, spread)


def slot_onehot(owner, devices, slots):
    n = owner.shape[1]
    mine = jnp.where(iota((devices, n), 0) == owner, 1.0, 0.0)
    before = jnp.where(iota((n, n), 0) < iota((n, n), 1), 1.0, 0.0).astype(BF16)
    count = dot(mine.astype(BF16), before)
    rank = jnp.sum(mine * count, axis=0, keepdims=True).astype(jnp.int32)
    target = owner * slots + rank
    return jnp.where(iota((devices * slots, n), 0) == target, 1.0, 0.0).astype(BF16)


def interleave_matrix():
    k, n = iota((512, 512), 0), iota((512, 512), 1)
    return jnp.where(n == EDGE * (k & 127) + (k >> 7), 1.0, 0.0).astype(BF16)


def velocity_of(c, psi, fac_ref, lanes):
    def f(i):
        return fac_ref[i : i + 1, lanes]

    if c == 0:
        return f(6) + f(0) * psi[0]
    if c == 1:
        return f(1) * psi[0] + f(2) * psi[1]
    return f(3) * psi[0] + f(4) * psi[1] + f(5) * psi[2]


def finish(c, strips, left_ref, right_ref, psi_ref, lanes_ref, hot_ref, interleave_ref, tile_ref, outgoing_ref):
    for g in range(8):
        lanes = slice(256 * g, 256 * g + 256)
        left, right = left_ref[c, :, lanes], right_ref[c, :, lanes]
        psi_c = psi_ref[c, :, lanes] + dot(strips, jnp.concatenate([left, right, left, right], axis=0))
        if c < 2:
            psi_ref[c, :, lanes] = psi_c
        psi = [psi_ref[i, :, lanes] for i in range(c)] + [psi_c]
        velocity = velocity_of(c, psi, lanes_ref, lanes).astype(BF16)
        for e in range(2):
            for dz in range(EDGE):
                tile_ref[32 * (2 * g + e) : 32 * (2 * g + e) + 32, 128 * dz : 128 * dz + 128] = velocity[
                    32 * dz : 32 * dz + 32, 128 * e : 128 * e + 128
                ]
    payload = dot(tile_ref[...], interleave_ref[...]).astype(BF16)
    for b in range(4):
        part = dot(hot_ref[256 * b : 256 * b + 256], payload)
        outgoing_ref[c, 32 * b : 32 * b + 32] = part.reshape(32, 8, 512).astype(BF16)


def kernel(
    n_span, n_wall, slots, wscale, sscale, noise_hbm, lund_ref, mean_ref, owner_ref, out_ref,
    noise_ref, low_ref, high_ref, smooth_ref, psi_ref, to_next_ref, to_prev_ref, left_ref, right_ref,
    fac_ref, lanes_ref, hot_ref, interleave_ref, tile_ref, outgoing_ref,
    load_sem, halo_send, halo_recv, strip_send, strip_recv, out_send, out_recv, self_sem, ready_sem,
):
    devices = n_span * n_wall
    span, wall = lax.axis_index("span"), lax.axis_index("wall")
    me = span * n_wall + wall
    rows = noise_hbm.shape[2]

    def place(index):
        return {"span": lax.div(index, n_wall), "wall": lax.rem(index, n_wall)}

    def greet(sem, axis, size, distance):
        here = lax.axis_index(axis)
        for step in (distance, size - distance):
            pl.semaphore_signal(sem, inc=1, device_id={axis: lax.rem(here + step, size)}, device_id_type=MESH)

    barrier = pltpu.get_barrier_semaphore()
    greet(barrier, "wall", n_wall, 1)
    greet(barrier, "span", n_span, 1)

    loads = [pltpu.make_async_copy(noise_hbm.at[c], noise_ref.at[c], load_sem.at[c]) for c in range(3)]
    for load in loads:
        load.start()

    def sends(c, step, size, axis, pairs, send_sem, recv_sem):
        here = lax.axis_index(axis)
        targets = (lax.rem(here + 1, size), lax.rem(here + size - 1, size))
        return [
            pltpu.make_async_remote_copy(
                src_ref=src, dst_ref=dst, send_sem=send_sem.at[c, i], recv_sem=recv_sem.at[c, i],
                device_id={axis: targets[i]}, device_id_type=MESH,
            )
            for i, (src, dst) in enumerate(pairs)
        ]

    halos = [
        sends(
            c, 0, n_wall, "wall",
            (
                (noise_hbm.at[c, :, pl.ds(rows - HALO, HALO), :], low_ref.at[c]),
                (noise_hbm.at[c, :, pl.ds(0, HALO), :], high_ref.at[c]),
            ),
            halo_send, halo_recv,
        )
        for c in range(3)
    ]
    strips = [
        sends(
            c, 1, n_span, "span",
            ((to_next_ref.at[c], left_ref.at[c]), (to_prev_ref.at[c], right_ref.at[c])),
            strip_send, strip_recv,
        )
        for c in range(3)
    ]

    pl.semaphore_wait(barrier, 4)
    inner = (wall < n_wall - 1, wall > 0)
    fed = (wall > 0, wall < n_wall - 1)
    for c in range(3):
        for i in range(2):
            pl.when(inner[i])(halos[c][i].start)
    greet(ready_sem.at[0], "wall", n_wall, 1)
    greet(ready_sem.at[0], "span", n_span, 1)
    for i, ref in enumerate((low_ref, high_ref)):

        @pl.when(jnp.logical_not(fed[i]))
        def _(ref=ref):
            ref[...] = jnp.zeros_like(ref)

    fac_ref[...] = jnp.zeros_like(fac_ref)
    fac_ref[0:6] = lund_ref[...]
    fac_ref[6:7] = mean_ref[...]
    lanes_ref[...] = lane_factors(fac_ref[...])
    hot_ref[...] = slot_onehot(owner_ref[...], devices, slots)
    interleave_ref[...] = interleave_matrix()
    pl.semaphore_wait(ready_sem.at[0], 4)
    greet(ready_sem.at[1], "wall", n_wall, 2)
    greet(ready_sem.at[1], "span", n_span, 2)

    def early(c):
        operand = wall_operand(wscale[c], wall, n_wall)
        own, from_strips = span_operands(sscale[c])
        loads[c].wait()
        for i in range(2):
            pl.when(fed[i])(halos[c][i].wait_recv)
        wall_pass(c, noise_ref, low_ref, high_ref, operand, smooth_ref)
        span_own_pass(c, own, smooth_ref, psi_ref, to_next_ref, to_prev_ref)
        for copy in strips[c]:
            copy.start()
        return from_strips

    def late(c, from_strips):
        for copy in strips[c]:
            copy.wait_recv()
        finish(c, from_strips, left_ref, right_ref, psi_ref, lanes_ref, hot_ref, interleave_ref, tile_ref, outgoing_ref)
        lanes = pl.ds(512 * c, 512)
        if c == 0:
            pl.semaphore_wait(ready_sem.at[3], n_wall - 1)

        def deliver(i, carry):
            to = jnp.bitwise_xor(me, jnp.bitwise_and(37 * i, devices - 1))
            pltpu.make_async_remote_copy(
                src_ref=outgoing_ref.at[c, to], dst_ref=out_ref.at[me, :, lanes],
                send_sem=out_send.at[c], recv_sem=out_recv.at[c], device_id=place(to), device_id_type=MESH,
            ).start()
            return carry

        lax.fori_loop(1, devices, deliver, 0)
        pltpu.make_async_copy(outgoing_ref.at[c, me], out_ref.at[me, :, lanes], self_sem.at[c]).start()

    first = early(0)
    pl.semaphore_wait(ready_sem.at[1], 4)
    greet(ready_sem.at[2], "span", n_span, 4)
    second = early(1)
    pl.semaphore_wait(ready_sem.at[2], 2)
    for i in range(1, n_wall):
        pl.semaphore_signal(
            ready_sem.at[3], inc=1, device_id={"wall": lax.rem(wall + i, n_wall)}, device_id_type=MESH
        )
    third = early(2)
    late(0, first)
    late(1, second)
    late(2, third)

    others = pl.ds(0, devices - 1)
    for c in range(3):
        for i in range(2):
            pl.when(inner[i])(halos[c][i].wait_send)
            strips[c][i].wait_send()
        lanes = pl.ds(512 * c, 512)
        pltpu.make_async_copy(outgoing_ref.at[c, me], out_ref.at[me, :, lanes], self_sem.at[c]).wait()
        pltpu.make_async_copy(outgoing_ref.at[c, others], outgoing_ref.at[c, others], out_send.at[c]).wait()
        pltpu.make_async_copy(out_ref.at[others, :, lanes], out_ref.at[others, :, lanes], out_recv.at[c]).wait()


VMEM = pl.BlockSpec(memory_space=pltpu.VMEM)
SMEM = pl.BlockSpec(memory_space=pltpu.SMEM)
ANY = pl.BlockSpec(memory_space=pl.ANY)
MESH = pl.DeviceIdType.MESH


def per_device(noise, wall_scale, span_scale, lund_factor, mean_velocity, owner_map):
    n_span, n_wall = lax.axis_size("span"), lax.axis_size("wall")
    devices = n_span * n_wall
    slots = 8
    received = pl.pallas_call(
        functools.partial(kernel, n_span, n_wall, slots),
        out_shape=jax.ShapeDtypeStruct((devices, slots, 1536), BF16),
        in_specs=[SMEM, SMEM, ANY, VMEM, VMEM, VMEM],
        out_specs=ANY,
        scratch_shapes=[
            pltpu.VMEM(noise.shape, BF16),
            pltpu.VMEM((3, 32, HALO, 128), BF16),
            pltpu.VMEM((3, 32, HALO, 128), BF16),
            pltpu.VMEM((16, 16, 8, 128), F32),
            pltpu.VMEM((3, 128, 2048), F32),
            pltpu.VMEM((3, STRIP, 2048), BF16),
            pltpu.VMEM((3, STRIP, 2048), BF16),
            pltpu.VMEM((3, STRIP, 2048), BF16),
            pltpu.VMEM((3, STRIP, 2048), BF16),
            pltpu.VMEM((8, 64), F32),
            pltpu.VMEM((8, 2048), F32),
            pltpu.VMEM((devices * slots, 512), BF16),
            pltpu.VMEM((512, 512), BF16),
            pltpu.VMEM((512, 512), BF16),
            pltpu.VMEM((3, devices, slots, 512), BF16),
            pltpu.SemaphoreType.DMA((3,)),
            pltpu.SemaphoreType.DMA((3, 2)),
            pltpu.SemaphoreType.DMA((3, 2)),
            pltpu.SemaphoreType.DMA((3, 2)),
            pltpu.SemaphoreType.DMA((3, 2)),
            pltpu.SemaphoreType.DMA((3,)),
            pltpu.SemaphoreType.DMA((3,)),
            pltpu.SemaphoreType.DMA((3,)),
            pltpu.SemaphoreType.REGULAR((4,)),
        ],
        compiler_params=pltpu.CompilerParams(collective_id=0, has_side_effects=True, vmem_limit_bytes=60 << 20),
        name="inflow",
    )(
        wall_scale, span_scale, noise, lund_factor, mean_velocity.reshape(1, -1), owner_map.reshape(1, -1)
    )
    return received.reshape(1, devices * slots, -1)


def solution(mesh):
    return jax.shard_map(
        per_device,
        mesh=mesh,
        in_specs=(
            P(None, None, "wall", "span"),
            P(),
            P(),
            P(None, "wall"),
            P("wall"),
            P("wall", "span", None, None),
        ),
        out_specs=P(("span", "wall"), None, None),
        check_vma=False,
    )
```

```python
import functools
import math

import jax
import jax.numpy as jnp
from jax import lax
from jax.experimental import pallas as pl
from jax.experimental.pallas import tpu as pltpu
from jax.sharding import PartitionSpec as P

HALO = 24
EDGE = 4
F32 = jnp.float32
BF16 = jnp.bfloat16


def iota(shape, dim):
    return lax.broadcasted_iota(jnp.int32, shape, dim)


def split(x):
    hi = x.astype(BF16)
    return hi, (x - hi.astype(F32)).astype(BF16)


def dot(a, b):
    return jnp.dot(a, b, preferred_element_type=F32)


def dot_nt(a, b):
    return lax.dot_general(a, b, (((1,), (1,)), ((), ())), preferred_element_type=F32)


def tap_coefficients(scale):
    square = jnp.full((1, 128), scale, F32)
    square = square * square
    lane = iota((1, 128), 1)
    k = (lane - HALO).astype(F32)
    energy = jnp.where(lane <= 2 * HALO, jnp.exp(-math.pi * k * k / square), 0.0)
    norm = jnp.sqrt(jnp.sum(energy, axis=1, keepdims=True))
    return (math.pi / (2.0 * square))[:, :1], 1.0 / norm


def tap_values(offset, valid, coefficients):
    rate, gain = coefficients
    d = offset.astype(F32)
    inside = valid & (offset >= -HALO) & (offset <= HALO)
    return jnp.where(inside, jnp.exp(-(d * d) * rate) * gain, 0.0)


def wall_operand(scale, wall, n_wall):
    shape = (128, 224)
    r, k = iota(shape, 0), iota(shape, 1)
    y = EDGE * (r >> 3) + (r & 3)
    t = (r >> 2) & 1
    core, low = k < 128, k < 176
    j = jnp.where(low, k - 128, k - 176)
    t_halo = (j >= HALO).astype(jnp.int32)
    inner = j - HALO * t_halo
    t_col = jnp.where(core, k >> 6, t_halo)
    y_col = jnp.where(core, k & 63, jnp.where(low, inner - HALO, inner + 64))
    first = (wall > 0).astype(jnp.int32)
    last = (wall < n_wall - 1).astype(jnp.int32)
    present = jnp.where(core, 1, jnp.where(low, first, last)) > 0
    values = tap_values(y_col - y, (t == t_col) & present, tap_coefficients(scale))
    hi, lo = split(values)
    return jnp.concatenate([hi, lo], axis=0)


def span_operands(scale):
    coefficients = tap_coefficients(scale)
    shape = (128, 128)
    r, k = iota(shape, 0), iota(shape, 1)
    z = EDGE * (r & 31) + (r >> 5)
    hi, lo = split(tap_values(k - z, r >= 0, coefficients))
    row, col = iota((2 * HALO, 256), 0), iota((2 * HALO, 256), 1)
    source = jnp.where(row < HALO, 128 - HALO + row, row - HALO)
    own = jnp.concatenate(
        [
            jnp.concatenate([hi, hi], axis=1),
            jnp.concatenate([lo, jnp.zeros_like(lo)], axis=1),
            jnp.where(col == source, 1.0, 0.0).astype(BF16),
        ],
        axis=0,
    )
    shape = (128, 4 * HALO)
    r, k = iota(shape, 0), iota(shape, 1)
    z = EDGE * (r & 31) + (r >> 5)
    second = k >= 2 * HALO
    j = jnp.where(second, k - 2 * HALO, k)
    column = jnp.where(j >= HALO, 128 + j - HALO, j - HALO)
    hi, lo = split(tap_values(column - z, r >= 0, coefficients))
    return own, jnp.where(second, lo.astype(F32), hi.astype(F32)).astype(BF16)


def wall_pass(c, noise_ref, low_ref, high_ref, operand, smooth_ref):
    planes = noise_ref.shape[1]
    for q in range(planes // 4):
        blocks = []
        for p in (2 * q, 2 * q + 1):
            blocks.append(
                jnp.concatenate(
                    [
                        noise_ref[c, 2 * p : 2 * p + 2].reshape(128, 128),
                        low_ref[c, 2 * p : 2 * p + 2].reshape(2 * HALO, 128),
                        high_ref[c, 2 * p : 2 * p + 2].reshape(2 * HALO, 128),
                    ],
                    axis=0,
                )
            )
        both = dot(operand, jnp.concatenate(blocks, axis=1))
        both = both[:128] + both[128:]
        smooth_ref[:, 2 * q] = both[:, :128].reshape(16, 8, 128)
        smooth_ref[:, 2 * q + 1] = both[:, 128:].reshape(16, 8, 128)


def span_own_pass(c, own, smooth_ref, psi_ref, to_next_ref, to_prev_ref):
    for g in range(8):
        hi, lo = split(smooth_ref[2 * g : 2 * g + 2].reshape(256, 128))
        out = dot_nt(own, jnp.concatenate([hi, lo], axis=1))
        lanes = slice(256 * g, 256 * g + 256)
        psi_ref[c, :, lanes] = out[:128] + out[128:256]
        to_next_ref[c, :, lanes] = out[256 : 256 + HALO].astype(BF16)
        to_prev_ref[c, :, lanes] = out[256 + HALO :].astype(BF16)


def lane_factors(fac):
    first, rest = fac.astype(BF16), None
    rest = fac - first.astype(F32)
    second = rest.astype(BF16)
    third = (rest - second.astype(F32)).astype(BF16)
    lane = iota((64, 2048), 1)
    spread = jnp.where(iota((64, 2048), 0) == EDGE * (lane >> 7) + (lane & 3), 1.0, 0.0).astype(BF16)
    return dot(first, spread) + dot(second, spread) + dot(third, spread)


def slot_onehot(owner, devices, slots):
    n = owner.shape[1]
    mine = jnp.where(iota((devices, n), 0) == owner, 1.0, 0.0)
    before = jnp.where(iota((n, n), 0) < iota((n, n), 1), 1.0, 0.0).astype(BF16)
    count = dot(mine.astype(BF16), before)
    rank = jnp.sum(mine * count, axis=0, keepdims=True).astype(jnp.int32)
    target = owner * slots + rank
    return jnp.where(iota((devices * slots, n), 0) == target, 1.0, 0.0).astype(BF16)


def interleave_matrix():
    k, n = iota((512, 512), 0), iota((512, 512), 1)
    return jnp.where(n == EDGE * (k & 127) + (k >> 7), 1.0, 0.0).astype(BF16)


def velocity_of(c, psi, fac_ref, lanes):
    def f(i):
        return fac_ref[i : i + 1, lanes]

    if c == 0:
        return f(6) + f(0) * psi[0]
    if c == 1:
        return f(1) * psi[0] + f(2) * psi[1]
    return f(3) * psi[0] + f(4) * psi[1] + f(5) * psi[2]


def finish(c, strips, left_ref, right_ref, psi_ref, lanes_ref, hot_ref, interleave_ref, tile_ref, outgoing_ref):
    for g in range(8):
        lanes = slice(256 * g, 256 * g + 256)
        left, right = left_ref[c, :, lanes], right_ref[c, :, lanes]
        psi_c = psi_ref[c, :, lanes] + dot(strips, jnp.concatenate([left, right, left, right], axis=0))
        if c < 2:
            psi_ref[c, :, lanes] = psi_c
        psi = [psi_ref[i, :, lanes] for i in range(c)] + [psi_c]
        velocity = velocity_of(c, psi, lanes_ref, lanes).astype(BF16)
        for e in range(2):
            for dz in range(EDGE):
                tile_ref[32 * (2 * g + e) : 32 * (2 * g + e) + 32, 128 * dz : 128 * dz + 128] = velocity[
                    32 * dz : 32 * dz + 32, 128 * e : 128 * e + 128
                ]
    payload = dot(tile_ref[...], interleave_ref[...]).astype(BF16)
    for b in range(4):
        part = dot(hot_ref[256 * b : 256 * b + 256], payload)
        outgoing_ref[c, 32 * b : 32 * b + 32] = part.reshape(32, 8, 512).astype(BF16)


def kernel(
    n_span, n_wall, slots, wscale, sscale, noise_hbm, lund_ref, mean_ref, owner_ref, out_ref,
    noise_ref, low_ref, high_ref, smooth_ref, psi_ref, to_next_ref, to_prev_ref, left_ref, right_ref,
    fac_ref, lanes_ref, hot_ref, interleave_ref, tile_ref, outgoing_ref,
    load_sem, halo_send, halo_recv, strip_send, strip_recv, out_send, out_recv, self_sem, ready_sem,
):
    devices = n_span * n_wall
    span, wall = lax.axis_index("span"), lax.axis_index("wall")
    me = span * n_wall + wall
    rows = noise_hbm.shape[2]

    def place(index):
        return {"span": lax.div(index, n_wall), "wall": lax.rem(index, n_wall)}

    def greet(sem, axis, size, distance):
        here = lax.axis_index(axis)
        for step in (distance, size - distance):
            pl.semaphore_signal(sem, inc=1, device_id={axis: lax.rem(here + step, size)}, device_id_type=MESH)

    barrier = pltpu.get_barrier_semaphore()
    greet(barrier, "wall", n_wall, 1)
    greet(barrier, "span", n_span, 1)

    loads = [pltpu.make_async_copy(noise_hbm.at[c], noise_ref.at[c], load_sem.at[c]) for c in range(3)]
    for load in loads:
        load.start()

    def sends(c, step, size, axis, pairs, send_sem, recv_sem):
        here = lax.axis_index(axis)
        targets = (lax.rem(here + 1, size), lax.rem(here + size - 1, size))
        return [
            pltpu.make_async_remote_copy(
                src_ref=src, dst_ref=dst, send_sem=send_sem.at[c, i], recv_sem=recv_sem.at[c, i],
                device_id={axis: targets[i]}, device_id_type=MESH,
            )
            for i, (src, dst) in enumerate(pairs)
        ]

    halos = [
        sends(
            c, 0, n_wall, "wall",
            (
                (noise_hbm.at[c, :, pl.ds(rows - HALO, HALO), :], low_ref.at[c]),
                (noise_hbm.at[c, :, pl.ds(0, HALO), :], high_ref.at[c]),
            ),
            halo_send, halo_recv,
        )
        for c in range(3)
    ]
    strips = [
        sends(
            c, 1, n_span, "span",
            ((to_next_ref.at[c], left_ref.at[c]), (to_prev_ref.at[c], right_ref.at[c])),
            strip_send, strip_recv,
        )
        for c in range(3)
    ]

    pl.semaphore_wait(barrier, 4)
    inner = (wall < n_wall - 1, wall > 0)
    fed = (wall > 0, wall < n_wall - 1)
    for c in range(3):
        for i in range(2):
            pl.when(inner[i])(halos[c][i].start)
    greet(ready_sem.at[0], "wall", n_wall, 1)
    greet(ready_sem.at[0], "span", n_span, 1)
    for i, ref in enumerate((low_ref, high_ref)):

        @pl.when(jnp.logical_not(fed[i]))
        def _(ref=ref):
            ref[...] = jnp.zeros_like(ref)

    fac_ref[...] = jnp.zeros_like(fac_ref)
    fac_ref[0:6] = lund_ref[...]
    fac_ref[6:7] = mean_ref[...]
    lanes_ref[...] = lane_factors(fac_ref[...])
    hot_ref[...] = slot_onehot(owner_ref[...], devices, slots)
    interleave_ref[...] = interleave_matrix()
    pl.semaphore_wait(ready_sem.at[0], 4)
    greet(ready_sem.at[1], "wall", n_wall, 2)
    greet(ready_sem.at[1], "span", n_span, 2)

    def early(c):
        operand = wall_operand(wscale[c], wall, n_wall)
        own, from_strips = span_operands(sscale[c])
        loads[c].wait()
        for i in range(2):
            pl.when(fed[i])(halos[c][i].wait_recv)
        wall_pass(c, noise_ref, low_ref, high_ref, operand, smooth_ref)
        span_own_pass(c, own, smooth_ref, psi_ref, to_next_ref, to_prev_ref)
        for copy in strips[c]:
            copy.start()
        return from_strips

    def late(c, from_strips):
        for copy in strips[c]:
            copy.wait_recv()
        finish(c, from_strips, left_ref, right_ref, psi_ref, lanes_ref, hot_ref, interleave_ref, tile_ref, outgoing_ref)
        lanes = pl.ds(512 * c, 512)
        if c == 0:
            pl.semaphore_wait(ready_sem.at[3], n_wall - 1)

        def deliver(i, carry):
            to = jnp.bitwise_xor(me, jnp.bitwise_and(43 * i, devices - 1))
            pltpu.make_async_remote_copy(
                src_ref=outgoing_ref.at[c, to], dst_ref=out_ref.at[me, :, lanes],
                send_sem=out_send.at[c], recv_sem=out_recv.at[c], device_id=place(to), device_id_type=MESH,
            ).start()
            return carry

        lax.fori_loop(1, devices, deliver, 0)
        pltpu.make_async_copy(outgoing_ref.at[c, me], out_ref.at[me, :, lanes], self_sem.at[c]).start()

    first = early(0)
    pl.semaphore_wait(ready_sem.at[1], 4)
    greet(ready_sem.at[2], "span", n_span, 4)
    second = early(1)
    pl.semaphore_wait(ready_sem.at[2], 2)
    for i in range(1, n_wall):
        pl.semaphore_signal(
            ready_sem.at[3], inc=1, device_id={"wall": lax.rem(wall + i, n_wall)}, device_id_type=MESH
        )
    third = early(2)
    late(0, first)
    late(1, second)
    late(2, third)

    others = pl.ds(0, devices - 1)
    for c in range(3):
        for i in range(2):
            pl.when(inner[i])(halos[c][i].wait_send)
            strips[c][i].wait_send()
        lanes = pl.ds(512 * c, 512)
        pltpu.make_async_copy(outgoing_ref.at[c, me], out_ref.at[me, :, lanes], self_sem.at[c]).wait()
        pltpu.make_async_copy(outgoing_ref.at[c, others], outgoing_ref.at[c, others], out_send.at[c]).wait()
        pltpu.make_async_copy(out_ref.at[others, :, lanes], out_ref.at[others, :, lanes], out_recv.at[c]).wait()


VMEM = pl.BlockSpec(memory_space=pltpu.VMEM)
SMEM = pl.BlockSpec(memory_space=pltpu.SMEM)
ANY = pl.BlockSpec(memory_space=pl.ANY)
MESH = pl.DeviceIdType.MESH


def per_device(noise, wall_scale, span_scale, lund_factor, mean_velocity, owner_map):
    n_span, n_wall = lax.axis_size("span"), lax.axis_size("wall")
    devices = n_span * n_wall
    slots = 8
    received = pl.pallas_call(
        functools.partial(kernel, n_span, n_wall, slots),
        out_shape=jax.ShapeDtypeStruct((devices, slots, 1536), BF16),
        in_specs=[SMEM, SMEM, ANY, VMEM, VMEM, VMEM],
        out_specs=ANY,
        scratch_shapes=[
            pltpu.VMEM(noise.shape, BF16),
            pltpu.VMEM((3, 32, HALO, 128), BF16),
            pltpu.VMEM((3, 32, HALO, 128), BF16),
            pltpu.VMEM((16, 16, 8, 128), F32),
            pltpu.VMEM((3, 128, 2048), F32),
            pltpu.VMEM((3, HALO, 2048), BF16),
            pltpu.VMEM((3, HALO, 2048), BF16),
            pltpu.VMEM((3, HALO, 2048), BF16),
            pltpu.VMEM((3, HALO, 2048), BF16),
            pltpu.VMEM((8, 64), F32),
            pltpu.VMEM((8, 2048), F32),
            pltpu.VMEM((devices * slots, 512), BF16),
            pltpu.VMEM((512, 512), BF16),
            pltpu.VMEM((512, 512), BF16),
            pltpu.VMEM((3, devices, slots, 512), BF16),
            pltpu.SemaphoreType.DMA((3,)),
            pltpu.SemaphoreType.DMA((3, 2)),
            pltpu.SemaphoreType.DMA((3, 2)),
            pltpu.SemaphoreType.DMA((3, 2)),
            pltpu.SemaphoreType.DMA((3, 2)),
            pltpu.SemaphoreType.DMA((3,)),
            pltpu.SemaphoreType.DMA((3,)),
            pltpu.SemaphoreType.DMA((3,)),
            pltpu.SemaphoreType.REGULAR((4,)),
        ],
        compiler_params=pltpu.CompilerParams(collective_id=0, has_side_effects=True, vmem_limit_bytes=60 << 20),
        name="inflow",
    )(
        wall_scale, span_scale, noise, lund_factor, mean_velocity.reshape(1, -1), owner_map.reshape(1, -1)
    )
    return received.reshape(1, devices * slots, -1)


def solution(mesh):
    return jax.shard_map(
        per_device,
        mesh=mesh,
        in_specs=(
            P(None, None, "wall", "span"),
            P(),
            P(),
            P(None, "wall"),
            P("wall"),
            P("wall", "span", None, None),
        ),
        out_specs=P(("span", "wall"), None, None),
        check_vma=False,
    )
```

```python
import functools
import math

import jax
import jax.numpy as jnp
from jax import lax
from jax.experimental import pallas as pl
from jax.experimental.pallas import tpu as pltpu
from jax.sharding import PartitionSpec as P

HALO = 24
EDGE = 4
STRIP = 32
F32 = jnp.float32
BF16 = jnp.bfloat16


def iota(shape, dim):
    return lax.broadcasted_iota(jnp.int32, shape, dim)


def split(x):
    hi = x.astype(BF16)
    return hi, (x - hi.astype(F32)).astype(BF16)


def dot(a, b):
    return jnp.dot(a, b, preferred_element_type=F32)


def dot_nt(a, b):
    return lax.dot_general(a, b, (((1,), (1,)), ((), ())), preferred_element_type=F32)


def tap_coefficients(scale):
    square = jnp.full((1, 128), scale, F32)
    square = square * square
    lane = iota((1, 128), 1)
    k = (lane - HALO).astype(F32)
    energy = jnp.where(lane <= 2 * HALO, jnp.exp(-math.pi * k * k / square), 0.0)
    norm = jnp.sqrt(jnp.sum(energy, axis=1, keepdims=True))
    return (math.pi / (2.0 * square))[:, :1], 1.0 / norm


def tap_values(offset, valid, coefficients):
    rate, gain = coefficients
    d = offset.astype(F32)
    inside = valid & (offset >= -HALO) & (offset <= HALO)
    return jnp.where(inside, jnp.exp(-(d * d) * rate) * gain, 0.0)


def wall_operand(scale, wall, n_wall):
    shape = (128, 224)
    r, k = iota(shape, 0), iota(shape, 1)
    y = EDGE * (r >> 3) + (r & 3)
    t = (r >> 2) & 1
    core, low = k < 128, k < 176
    j = jnp.where(low, k - 128, k - 176)
    t_halo = (j >= HALO).astype(jnp.int32)
    inner = j - HALO * t_halo
    t_col = jnp.where(core, k >> 6, t_halo)
    y_col = jnp.where(core, k & 63, jnp.where(low, inner - HALO, inner + 64))
    first = (wall > 0).astype(jnp.int32)
    last = (wall < n_wall - 1).astype(jnp.int32)
    present = jnp.where(core, 1, jnp.where(low, first, last)) > 0
    values = tap_values(y_col - y, (t == t_col) & present, tap_coefficients(scale))
    hi, lo = split(values)
    return jnp.concatenate([hi, lo], axis=0)


def span_operands(scale):
    coefficients = tap_coefficients(scale)
    shape = (128, 128)
    r, k = iota(shape, 0), iota(shape, 1)
    z = EDGE * (r & 31) + (r >> 5)
    hi, lo = split(tap_values(k - z, r >= 0, coefficients))
    row, col = iota((2 * STRIP, 256), 0), iota((2 * STRIP, 256), 1)
    j = row & (STRIP - 1)
    low_term = j >= HALO
    to_next = jnp.where(low_term, 256 - STRIP + j, 128 - HALO + j)
    to_prev = jnp.where(low_term, 128 - HALO + j, j)
    pick = jnp.where(col == jnp.where(row < STRIP, to_next, to_prev), 1.0, 0.0).astype(BF16)
    own = jnp.concatenate(
        [
            jnp.concatenate([hi, hi], axis=1),
            jnp.concatenate([lo, jnp.zeros_like(lo)], axis=1),
            pick,
        ],
        axis=0,
    )
    second = k >= 2 * STRIP
    j = k & (STRIP - 1)
    low_term = j >= HALO
    from_left = jnp.where(low_term, j - STRIP, j - HALO)
    from_right = jnp.where(low_term, 128 + j - HALO, 128 + j)
    column = jnp.where((k & STRIP) > 0, from_right, from_left)
    values = tap_values(column - z, r >= 0, coefficients)
    hi = values.astype(BF16).astype(F32)
    strips = jnp.where(second, jnp.where(low_term, 0.0, values - hi), hi).astype(BF16)
    return own, strips


def wall_pass(c, noise_ref, low_ref, high_ref, operand, smooth_ref):
    planes = noise_ref.shape[1]
    for q in range(planes // 4):
        blocks = []
        for p in (2 * q, 2 * q + 1):
            blocks.append(
                jnp.concatenate(
                    [
                        noise_ref[c, 2 * p : 2 * p + 2].reshape(128, 128),
                        low_ref[c, 2 * p : 2 * p + 2].reshape(2 * HALO, 128),
                        high_ref[c, 2 * p : 2 * p + 2].reshape(2 * HALO, 128),
                    ],
                    axis=0,
                )
            )
        both = dot(operand, jnp.concatenate(blocks, axis=1))
        both = both[:128] + both[128:]
        smooth_ref[:, 2 * q] = both[:, :128].reshape(16, 8, 128)
        smooth_ref[:, 2 * q + 1] = both[:, 128:].reshape(16, 8, 128)


def span_own_pass(c, own, smooth_ref, psi_ref, to_next_ref, to_prev_ref):
    for g in range(8):
        hi, lo = split(smooth_ref[2 * g : 2 * g + 2].reshape(256, 128))
        out = dot_nt(own, jnp.concatenate([hi, lo], axis=1))
        lanes = slice(256 * g, 256 * g + 256)
        psi_ref[c, :, lanes] = out[:128] + out[128:256]
        to_next_ref[c, :, lanes] = out[256 : 256 + STRIP].astype(BF16)
        to_prev_ref[c, :, lanes] = out[256 + STRIP :].astype(BF16)


def lane_factors(fac):
    first, rest = fac.astype(BF16), None
    rest = fac - first.astype(F32)
    second = rest.astype(BF16)
    third = (rest - second.astype(F32)).astype(BF16)
    lane = iota((64, 2048), 1)
    spread = jnp.where(iota((64, 2048), 0) == EDGE * (lane >> 7) + (lane & 3), 1.0, 0.0).astype(BF16)
    return dot(first, spread) + dot(second, spread) + dot(third, spread)


def slot_onehot(owner, devices, slots):
    n = owner.shape[1]
    mine = jnp.where(iota((devices, n), 0) == owner, 1.0, 0.0)
    before = jnp.where(iota((n, n), 0) < iota((n, n), 1), 1.0, 0.0).astype(BF16)
    count = dot(mine.astype(BF16), before)
    rank = jnp.sum(mine * count, axis=0, keepdims=True).astype(jnp.int32)
    target = owner * slots + rank
    return jnp.where(iota((devices * slots, n), 0) == target, 1.0, 0.0).astype(BF16)


def interleave_matrix():
    k, n = iota((512, 512), 0), iota((512, 512), 1)
    return jnp.where(n == EDGE * (k & 127) + (k >> 7), 1.0, 0.0).astype(BF16)


def velocity_of(c, psi, fac_ref, lanes):
    def f(i):
        return fac_ref[i : i + 1, lanes]

    if c == 0:
        return f(6) + f(0) * psi[0]
    if c == 1:
        return f(1) * psi[0] + f(2) * psi[1]
    return f(3) * psi[0] + f(4) * psi[1] + f(5) * psi[2]


def finish(c, strips, left_ref, right_ref, psi_ref, lanes_ref, hot_ref, interleave_ref, tile_ref, outgoing_ref):
    for g in range(8):
        lanes = slice(256 * g, 256 * g + 256)
        left, right = left_ref[c, :, lanes], right_ref[c, :, lanes]
        psi_c = psi_ref[c, :, lanes] + dot(strips, jnp.concatenate([left, right, left, right], axis=0))
        if c < 2:
            psi_ref[c, :, lanes] = psi_c
        psi = [psi_ref[i, :, lanes] for i in range(c)] + [psi_c]
        velocity = velocity_of(c, psi, lanes_ref, lanes).astype(BF16)
        for e in range(2):
            for dz in range(EDGE):
                tile_ref[32 * (2 * g + e) : 32 * (2 * g + e) + 32, 128 * dz : 128 * dz + 128] = velocity[
                    32 * dz : 32 * dz + 32, 128 * e : 128 * e + 128
                ]
    payload = dot(tile_ref[...], interleave_ref[...]).astype(BF16)
    for b in range(4):
        part = dot(hot_ref[256 * b : 256 * b + 256], payload)
        outgoing_ref[c, 32 * b : 32 * b + 32] = part.reshape(32, 8, 512).astype(BF16)


def kernel(
    n_span, n_wall, slots, wscale, sscale, noise_hbm, lund_ref, mean_ref, owner_ref, out_ref,
    noise_ref, low_ref, high_ref, smooth_ref, psi_ref, to_next_ref, to_prev_ref, left_ref, right_ref,
    fac_ref, lanes_ref, hot_ref, interleave_ref, tile_ref, outgoing_ref,
    load_sem, halo_send, halo_recv, strip_send, strip_recv, out_send, out_recv, self_sem, ready_sem,
):
    devices = n_span * n_wall
    span, wall = lax.axis_index("span"), lax.axis_index("wall")
    me = span * n_wall + wall
    rows = noise_hbm.shape[2]

    def place(index):
        return {"span": lax.div(index, n_wall), "wall": lax.rem(index, n_wall)}

    def greet(sem, axis, size, distance):
        here = lax.axis_index(axis)
        for step in (distance, size - distance):
            pl.semaphore_signal(sem, inc=1, device_id={axis: lax.rem(here + step, size)}, device_id_type=MESH)

    barrier = pltpu.get_barrier_semaphore()
    greet(barrier, "wall", n_wall, 1)
    greet(barrier, "span", n_span, 1)

    loads = [pltpu.make_async_copy(noise_hbm.at[c], noise_ref.at[c], load_sem.at[c]) for c in range(3)]
    for load in loads:
        load.start()

    def sends(c, step, size, axis, pairs, send_sem, recv_sem):
        here = lax.axis_index(axis)
        targets = (lax.rem(here + 1, size), lax.rem(here + size - 1, size))
        return [
            pltpu.make_async_remote_copy(
                src_ref=src, dst_ref=dst, send_sem=send_sem.at[c, i], recv_sem=recv_sem.at[c, i],
                device_id={axis: targets[i]}, device_id_type=MESH,
            )
            for i, (src, dst) in enumerate(pairs)
        ]

    halos = [
        sends(
            c, 0, n_wall, "wall",
            (
                (noise_hbm.at[c, :, pl.ds(rows - HALO, HALO), :], low_ref.at[c]),
                (noise_hbm.at[c, :, pl.ds(0, HALO), :], high_ref.at[c]),
            ),
            halo_send, halo_recv,
        )
        for c in range(3)
    ]
    strips = [
        sends(
            c, 1, n_span, "span",
            ((to_next_ref.at[c], left_ref.at[c]), (to_prev_ref.at[c], right_ref.at[c])),
            strip_send, strip_recv,
        )
        for c in range(3)
    ]

    pl.semaphore_wait(barrier, 4)
    inner = (wall < n_wall - 1, wall > 0)
    fed = (wall > 0, wall < n_wall - 1)
    for c in range(3):
        for i in range(2):
            pl.when(inner[i])(halos[c][i].start)
    greet(ready_sem.at[0], "wall", n_wall, 1)
    greet(ready_sem.at[0], "span", n_span, 1)
    for i, ref in enumerate((low_ref, high_ref)):

        @pl.when(jnp.logical_not(fed[i]))
        def _(ref=ref):
            ref[...] = jnp.zeros_like(ref)

    fac_ref[...] = jnp.zeros_like(fac_ref)
    fac_ref[0:6] = lund_ref[...]
    fac_ref[6:7] = mean_ref[...]
    lanes_ref[...] = lane_factors(fac_ref[...])
    hot_ref[...] = slot_onehot(owner_ref[...], devices, slots)
    interleave_ref[...] = interleave_matrix()
    pl.semaphore_wait(ready_sem.at[0], 4)
    greet(ready_sem.at[1], "wall", n_wall, 2)
    greet(ready_sem.at[1], "span", n_span, 2)

    def early(c):
        operand = wall_operand(wscale[c], wall, n_wall)
        own, from_strips = span_operands(sscale[c])
        loads[c].wait()
        for i in range(2):
            pl.when(fed[i])(halos[c][i].wait_recv)
        wall_pass(c, noise_ref, low_ref, high_ref, operand, smooth_ref)
        span_own_pass(c, own, smooth_ref, psi_ref, to_next_ref, to_prev_ref)
        for copy in strips[c]:
            copy.start()
        return from_strips

    def late(c, from_strips):
        for copy in strips[c]:
            copy.wait_recv()
        finish(c, from_strips, left_ref, right_ref, psi_ref, lanes_ref, hot_ref, interleave_ref, tile_ref, outgoing_ref)
        lanes = pl.ds(512 * c, 512)
        if c == 0:
            pl.semaphore_wait(ready_sem.at[3], n_wall - 1)

        def deliver(i, carry):
            to = jnp.bitwise_xor(me, jnp.bitwise_and(43 * i, devices - 1))
            pltpu.make_async_remote_copy(
                src_ref=outgoing_ref.at[c, to], dst_ref=out_ref.at[me, :, lanes],
                send_sem=out_send.at[c], recv_sem=out_recv.at[c], device_id=place(to), device_id_type=MESH,
            ).start()
            return carry

        lax.fori_loop(1, devices, deliver, 0)
        pltpu.make_async_copy(outgoing_ref.at[c, me], out_ref.at[me, :, lanes], self_sem.at[c]).start()

    first = early(0)
    pl.semaphore_wait(ready_sem.at[1], 4)
    greet(ready_sem.at[2], "span", n_span, 4)
    second = early(1)
    pl.semaphore_wait(ready_sem.at[2], 2)
    for i in range(1, n_wall):
        pl.semaphore_signal(
            ready_sem.at[3], inc=1, device_id={"wall": lax.rem(wall + i, n_wall)}, device_id_type=MESH
        )
    third = early(2)
    late(0, first)
    late(1, second)
    late(2, third)

    others = pl.ds(0, devices - 1)
    for c in range(3):
        for i in range(2):
            pl.when(inner[i])(halos[c][i].wait_send)
            strips[c][i].wait_send()
        lanes = pl.ds(512 * c, 512)
        pltpu.make_async_copy(outgoing_ref.at[c, me], out_ref.at[me, :, lanes], self_sem.at[c]).wait()
        pltpu.make_async_copy(outgoing_ref.at[c, others], outgoing_ref.at[c, others], out_send.at[c]).wait()
        pltpu.make_async_copy(out_ref.at[others, :, lanes], out_ref.at[others, :, lanes], out_recv.at[c]).wait()


VMEM = pl.BlockSpec(memory_space=pltpu.VMEM)
SMEM = pl.BlockSpec(memory_space=pltpu.SMEM)
ANY = pl.BlockSpec(memory_space=pl.ANY)
MESH = pl.DeviceIdType.MESH


def per_device(noise, wall_scale, span_scale, lund_factor, mean_velocity, owner_map):
    n_span, n_wall = lax.axis_size("span"), lax.axis_size("wall")
    devices = n_span * n_wall
    slots = 8
    received = pl.pallas_call(
        functools.partial(kernel, n_span, n_wall, slots),
        out_shape=jax.ShapeDtypeStruct((devices, slots, 1536), BF16),
        in_specs=[SMEM, SMEM, ANY, VMEM, VMEM, VMEM],
        out_specs=ANY,
        scratch_shapes=[
            pltpu.VMEM(noise.shape, BF16),
            pltpu.VMEM((3, 32, HALO, 128), BF16),
            pltpu.VMEM((3, 32, HALO, 128), BF16),
            pltpu.VMEM((16, 16, 8, 128), F32),
            pltpu.VMEM((3, 128, 2048), F32),
            pltpu.VMEM((3, STRIP, 2048), BF16),
            pltpu.VMEM((3, STRIP, 2048), BF16),
            pltpu.VMEM((3, STRIP, 2048), BF16),
            pltpu.VMEM((3, STRIP, 2048), BF16),
            pltpu.VMEM((8, 64), F32),
            pltpu.VMEM((8, 2048), F32),
            pltpu.VMEM((devices * slots, 512), BF16),
            pltpu.VMEM((512, 512), BF16),
            pltpu.VMEM((512, 512), BF16),
            pltpu.VMEM((3, devices, slots, 512), BF16),
            pltpu.SemaphoreType.DMA((3,)),
            pltpu.SemaphoreType.DMA((3, 2)),
            pltpu.SemaphoreType.DMA((3, 2)),
            pltpu.SemaphoreType.DMA((3, 2)),
            pltpu.SemaphoreType.DMA((3, 2)),
            pltpu.SemaphoreType.DMA((3,)),
            pltpu.SemaphoreType.DMA((3,)),
            pltpu.SemaphoreType.DMA((3,)),
            pltpu.SemaphoreType.REGULAR((4,)),
        ],
        compiler_params=pltpu.CompilerParams(collective_id=0, has_side_effects=True, vmem_limit_bytes=60 << 20),
        name="inflow",
    )(
        wall_scale, span_scale, noise, lund_factor, mean_velocity.reshape(1, -1), owner_map.reshape(1, -1)
    )
    return received.reshape(1, devices * slots, -1)


def solution(mesh):
    return jax.shard_map(
        per_device,
        mesh=mesh,
        in_specs=(
            P(None, None, "wall", "span"),
            P(),
            P(),
            P(None, "wall"),
            P("wall"),
            P("wall", "span", None, None),
        ),
        out_specs=P(("span", "wall"), None, None),
        check_vma=False,
    )
```

```python
import functools
import math

import jax
import jax.numpy as jnp
from jax import lax
from jax.experimental import pallas as pl
from jax.experimental.pallas import tpu as pltpu
from jax.sharding import PartitionSpec as P

HALO = 24
EDGE = 4
F32 = jnp.float32
BF16 = jnp.bfloat16


def iota(shape, dim):
    return lax.broadcasted_iota(jnp.int32, shape, dim)


def split(x):
    hi = x.astype(BF16)
    return hi, (x - hi.astype(F32)).astype(BF16)


def dot(a, b):
    return jnp.dot(a, b, preferred_element_type=F32)


def dot_nt(a, b):
    return lax.dot_general(a, b, (((1,), (1,)), ((), ())), preferred_element_type=F32)


def tap_coefficients(scale):
    square = jnp.full((1, 128), scale, F32)
    square = square * square
    lane = iota((1, 128), 1)
    k = (lane - HALO).astype(F32)
    energy = jnp.where(lane <= 2 * HALO, jnp.exp(-math.pi * k * k / square), 0.0)
    norm = jnp.sqrt(jnp.sum(energy, axis=1, keepdims=True))
    return (math.pi / (2.0 * square))[:, :1], 1.0 / norm


def tap_values(offset, valid, coefficients):
    rate, gain = coefficients
    d = offset.astype(F32)
    inside = valid & (offset >= -HALO) & (offset <= HALO)
    return jnp.where(inside, jnp.exp(-(d * d) * rate) * gain, 0.0)


def wall_operand(scale, wall, n_wall):
    shape = (128, 224)
    r, k = iota(shape, 0), iota(shape, 1)
    y = EDGE * (r >> 3) + (r & 3)
    t = (r >> 2) & 1
    core, low = k < 128, k < 176
    j = jnp.where(low, k - 128, k - 176)
    t_halo = (j >= HALO).astype(jnp.int32)
    inner = j - HALO * t_halo
    t_col = jnp.where(core, k >> 6, t_halo)
    y_col = jnp.where(core, k & 63, jnp.where(low, inner - HALO, inner + 64))
    first = (wall > 0).astype(jnp.int32)
    last = (wall < n_wall - 1).astype(jnp.int32)
    present = jnp.where(core, 1, jnp.where(low, first, last)) > 0
    values = tap_values(y_col - y, (t == t_col) & present, tap_coefficients(scale))
    hi, lo = split(values)
    return jnp.concatenate([hi, lo], axis=0)


def span_operands(scale):
    coefficients = tap_coefficients(scale)
    shape = (128, 128)
    r, k = iota(shape, 0), iota(shape, 1)
    z = EDGE * (r & 31) + (r >> 5)
    hi, lo = split(tap_values(k - z, r >= 0, coefficients))
    row, col = iota((2 * HALO, 256), 0), iota((2 * HALO, 256), 1)
    source = jnp.where(row < HALO, 128 - HALO + row, row - HALO)
    own = jnp.concatenate(
        [
            jnp.concatenate([hi, hi], axis=1),
            jnp.concatenate([lo, jnp.zeros_like(lo)], axis=1),
            jnp.where(col == source, 1.0, 0.0).astype(BF16),
        ],
        axis=0,
    )
    shape = (128, 4 * HALO)
    r, k = iota(shape, 0), iota(shape, 1)
    z = EDGE * (r & 31) + (r >> 5)
    second = k >= 2 * HALO
    j = jnp.where(second, k - 2 * HALO, k)
    column = jnp.where(j >= HALO, 128 + j - HALO, j - HALO)
    hi, lo = split(tap_values(column - z, r >= 0, coefficients))
    return own, jnp.where(second, lo.astype(F32), hi.astype(F32)).astype(BF16)


def wall_pass(c, noise_ref, low_ref, high_ref, operand, smooth_ref):
    planes = noise_ref.shape[1]
    for q in range(planes // 4):
        blocks = []
        for p in (2 * q, 2 * q + 1):
            blocks.append(
                jnp.concatenate(
                    [
                        noise_ref[c, 2 * p : 2 * p + 2].reshape(128, 128),
                        low_ref[c, 2 * p : 2 * p + 2].reshape(2 * HALO, 128),
                        high_ref[c, 2 * p : 2 * p + 2].reshape(2 * HALO, 128),
                    ],
                    axis=0,
                )
            )
        both = dot(operand, jnp.concatenate(blocks, axis=1))
        both = both[:128] + both[128:]
        smooth_ref[:, 2 * q] = both[:, :128].reshape(16, 8, 128)
        smooth_ref[:, 2 * q + 1] = both[:, 128:].reshape(16, 8, 128)


def span_own_pass(c, own, smooth_ref, psi_ref, to_next_ref, to_prev_ref):
    for g in range(8):
        hi, lo = split(smooth_ref[2 * g : 2 * g + 2].reshape(256, 128))
        out = dot_nt(own, jnp.concatenate([hi, lo], axis=1))
        lanes = slice(256 * g, 256 * g + 256)
        psi_ref[c, :, lanes] = out[:128] + out[128:256]
        to_next_ref[c, :, lanes] = out[256 : 256 + HALO].astype(BF16)
        to_prev_ref[c, :, lanes] = out[256 + HALO :].astype(BF16)


def lane_factors(fac):
    first, rest = fac.astype(BF16), None
    rest = fac - first.astype(F32)
    second = rest.astype(BF16)
    third = (rest - second.astype(F32)).astype(BF16)
    lane = iota((64, 2048), 1)
    spread = jnp.where(iota((64, 2048), 0) == EDGE * (lane >> 7) + (lane & 3), 1.0, 0.0).astype(BF16)
    return dot(first, spread) + dot(second, spread) + dot(third, spread)


def slot_onehot(owner, devices, slots):
    n = owner.shape[1]
    mine = jnp.where(iota((devices, n), 0) == owner, 1.0, 0.0)
    before = jnp.where(iota((n, n), 0) < iota((n, n), 1), 1.0, 0.0).astype(BF16)
    count = dot(mine.astype(BF16), before)
    rank = jnp.sum(mine * count, axis=0, keepdims=True).astype(jnp.int32)
    target = owner * slots + rank
    return jnp.where(iota((devices * slots, n), 0) == target, 1.0, 0.0).astype(BF16)


def interleave_matrix():
    k, n = iota((512, 512), 0), iota((512, 512), 1)
    return jnp.where(n == EDGE * (k & 127) + (k >> 7), 1.0, 0.0).astype(BF16)


def velocity_of(c, psi, fac_ref, lanes):
    def f(i):
        return fac_ref[i : i + 1, lanes]

    if c == 0:
        return f(6) + f(0) * psi[0]
    if c == 1:
        return f(1) * psi[0] + f(2) * psi[1]
    return f(3) * psi[0] + f(4) * psi[1] + f(5) * psi[2]


def finish(c, strips, left_ref, right_ref, psi_ref, lanes_ref, hot_ref, interleave_ref, tile_ref, outgoing_ref):
    for g in range(8):
        lanes = slice(256 * g, 256 * g + 256)
        left, right = left_ref[c, :, lanes], right_ref[c, :, lanes]
        psi_c = psi_ref[c, :, lanes] + dot(strips, jnp.concatenate([left, right, left, right], axis=0))
        if c < 2:
            psi_ref[c, :, lanes] = psi_c
        psi = [psi_ref[i, :, lanes] for i in range(c)] + [psi_c]
        velocity = velocity_of(c, psi, lanes_ref, lanes).astype(BF16)
        for e in range(2):
            for dz in range(EDGE):
                tile_ref[32 * (2 * g + e) : 32 * (2 * g + e) + 32, 128 * dz : 128 * dz + 128] = velocity[
                    32 * dz : 32 * dz + 32, 128 * e : 128 * e + 128
                ]
    payload = dot(tile_ref[...], interleave_ref[...]).astype(BF16)
    for b in range(4):
        part = dot(hot_ref[256 * b : 256 * b + 256], payload)
        outgoing_ref[c, 32 * b : 32 * b + 32] = part.reshape(32, 8, 512).astype(BF16)


def kernel(
    n_span, n_wall, slots, wscale, sscale, noise_hbm, lund_ref, mean_ref, owner_ref, out_ref,
    noise_ref, low_ref, high_ref, smooth_ref, psi_ref, to_next_ref, to_prev_ref, left_ref, right_ref,
    fac_ref, lanes_ref, hot_ref, interleave_ref, tile_ref, outgoing_ref,
    load_sem, halo_send, halo_recv, strip_send, strip_recv, out_send, out_recv, self_sem, ready_sem,
):
    devices = n_span * n_wall
    span, wall = lax.axis_index("span"), lax.axis_index("wall")
    me = span * n_wall + wall
    rows = noise_hbm.shape[2]

    def place(index):
        return {"span": index >> (n_wall.bit_length() - 1), "wall": jnp.bitwise_and(index, n_wall - 1)}

    def greet(sem, axis, size, distance):
        here = lax.axis_index(axis)
        for step in (distance, size - distance):
            pl.semaphore_signal(sem, inc=1, device_id={axis: lax.rem(here + step, size)}, device_id_type=MESH)

    barrier = pltpu.get_barrier_semaphore()
    greet(barrier, "wall", n_wall, 1)
    greet(barrier, "span", n_span, 1)

    loads = [pltpu.make_async_copy(noise_hbm.at[c], noise_ref.at[c], load_sem.at[c]) for c in range(3)]
    for load in loads:
        load.start()

    def sends(c, step, size, axis, pairs, send_sem, recv_sem):
        here = lax.axis_index(axis)
        targets = (lax.rem(here + 1, size), lax.rem(here + size - 1, size))
        return [
            pltpu.make_async_remote_copy(
                src_ref=src, dst_ref=dst, send_sem=send_sem.at[c, i], recv_sem=recv_sem.at[c, i],
                device_id={axis: targets[i]}, device_id_type=MESH,
            )
            for i, (src, dst) in enumerate(pairs)
        ]

    halos = [
        sends(
            c, 0, n_wall, "wall",
            (
                (noise_hbm.at[c, :, pl.ds(rows - HALO, HALO), :], low_ref.at[c]),
                (noise_hbm.at[c, :, pl.ds(0, HALO), :], high_ref.at[c]),
            ),
            halo_send, halo_recv,
        )
        for c in range(3)
    ]
    strips = [
        sends(
            c, 1, n_span, "span",
            ((to_next_ref.at[c], left_ref.at[c]), (to_prev_ref.at[c], right_ref.at[c])),
            strip_send, strip_recv,
        )
        for c in range(3)
    ]

    pl.semaphore_wait(barrier, 4)
    inner = (wall < n_wall - 1, wall > 0)
    fed = (wall > 0, wall < n_wall - 1)
    for c in range(3):
        for i in range(2):
            pl.when(inner[i])(halos[c][i].start)
    greet(ready_sem.at[0], "wall", n_wall, 1)
    greet(ready_sem.at[0], "span", n_span, 1)
    for i, ref in enumerate((low_ref, high_ref)):

        @pl.when(jnp.logical_not(fed[i]))
        def _(ref=ref):
            ref[...] = jnp.zeros_like(ref)

    fac_ref[...] = jnp.zeros_like(fac_ref)
    fac_ref[0:6] = lund_ref[...]
    fac_ref[6:7] = mean_ref[...]
    lanes_ref[...] = lane_factors(fac_ref[...])
    hot_ref[...] = slot_onehot(owner_ref[...], devices, slots)
    interleave_ref[...] = interleave_matrix()
    pl.semaphore_wait(ready_sem.at[0], 4)
    greet(ready_sem.at[1], "wall", n_wall, 2)
    greet(ready_sem.at[1], "span", n_span, 2)

    def early(c):
        operand = wall_operand(wscale[c], wall, n_wall)
        own, from_strips = span_operands(sscale[c])
        loads[c].wait()
        for i in range(2):
            pl.when(fed[i])(halos[c][i].wait_recv)
        wall_pass(c, noise_ref, low_ref, high_ref, operand, smooth_ref)
        span_own_pass(c, own, smooth_ref, psi_ref, to_next_ref, to_prev_ref)
        for copy in strips[c]:
            copy.start()
        return from_strips

    def late(c, from_strips):
        for copy in strips[c]:
            copy.wait_recv()
        finish(c, from_strips, left_ref, right_ref, psi_ref, lanes_ref, hot_ref, interleave_ref, tile_ref, outgoing_ref)
        lanes = pl.ds(512 * c, 512)
        if c == 0:
            pl.semaphore_wait(ready_sem.at[3], n_wall - 1)

        def deliver(i, carry):
            to = jnp.bitwise_xor(me, jnp.bitwise_and(43 * i, devices - 1))
            pltpu.make_async_remote_copy(
                src_ref=outgoing_ref.at[c, to], dst_ref=out_ref.at[me, :, lanes],
                send_sem=out_send.at[c], recv_sem=out_recv.at[c], device_id=place(to), device_id_type=MESH,
            ).start()
            return carry

        lax.fori_loop(1, devices, deliver, 0)
        pltpu.make_async_copy(outgoing_ref.at[c, me], out_ref.at[me, :, lanes], self_sem.at[c]).start()

    first = early(0)
    pl.semaphore_wait(ready_sem.at[1], 4)
    greet(ready_sem.at[2], "span", n_span, 4)
    second = early(1)
    pl.semaphore_wait(ready_sem.at[2], 2)
    for i in range(1, n_wall):
        pl.semaphore_signal(
            ready_sem.at[3], inc=1, device_id={"wall": lax.rem(wall + i, n_wall)}, device_id_type=MESH
        )
    third = early(2)
    late(0, first)
    late(1, second)
    late(2, third)

    others = pl.ds(0, devices - 1)
    for c in range(3):
        for i in range(2):
            pl.when(inner[i])(halos[c][i].wait_send)
            strips[c][i].wait_send()
        lanes = pl.ds(512 * c, 512)
        pltpu.make_async_copy(outgoing_ref.at[c, me], out_ref.at[me, :, lanes], self_sem.at[c]).wait()
        pltpu.make_async_copy(outgoing_ref.at[c, others], outgoing_ref.at[c, others], out_send.at[c]).wait()
        pltpu.make_async_copy(out_ref.at[others, :, lanes], out_ref.at[others, :, lanes], out_recv.at[c]).wait()


VMEM = pl.BlockSpec(memory_space=pltpu.VMEM)
SMEM = pl.BlockSpec(memory_space=pltpu.SMEM)
ANY = pl.BlockSpec(memory_space=pl.ANY)
MESH = pl.DeviceIdType.MESH


def per_device(noise, wall_scale, span_scale, lund_factor, mean_velocity, owner_map):
    n_span, n_wall = lax.axis_size("span"), lax.axis_size("wall")
    devices = n_span * n_wall
    slots = 8
    received = pl.pallas_call(
        functools.partial(kernel, n_span, n_wall, slots),
        out_shape=jax.ShapeDtypeStruct((devices, slots, 1536), BF16),
        in_specs=[SMEM, SMEM, ANY, VMEM, VMEM, VMEM],
        out_specs=ANY,
        scratch_shapes=[
            pltpu.VMEM(noise.shape, BF16),
            pltpu.VMEM((3, 32, HALO, 128), BF16),
            pltpu.VMEM((3, 32, HALO, 128), BF16),
            pltpu.VMEM((16, 16, 8, 128), F32),
            pltpu.VMEM((3, 128, 2048), F32),
            pltpu.VMEM((3, HALO, 2048), BF16),
            pltpu.VMEM((3, HALO, 2048), BF16),
            pltpu.VMEM((3, HALO, 2048), BF16),
            pltpu.VMEM((3, HALO, 2048), BF16),
            pltpu.VMEM((8, 64), F32),
            pltpu.VMEM((8, 2048), F32),
            pltpu.VMEM((devices * slots, 512), BF16),
            pltpu.VMEM((512, 512), BF16),
            pltpu.VMEM((512, 512), BF16),
            pltpu.VMEM((3, devices, slots, 512), BF16),
            pltpu.SemaphoreType.DMA((3,)),
            pltpu.SemaphoreType.DMA((3, 2)),
            pltpu.SemaphoreType.DMA((3, 2)),
            pltpu.SemaphoreType.DMA((3, 2)),
            pltpu.SemaphoreType.DMA((3, 2)),
            pltpu.SemaphoreType.DMA((3,)),
            pltpu.SemaphoreType.DMA((3,)),
            pltpu.SemaphoreType.DMA((3,)),
            pltpu.SemaphoreType.REGULAR((4,)),
        ],
        compiler_params=pltpu.CompilerParams(collective_id=0, has_side_effects=True, vmem_limit_bytes=60 << 20),
        name="inflow",
    )(
        wall_scale, span_scale, noise, lund_factor, mean_velocity.reshape(1, -1), owner_map.reshape(1, -1)
    )
    return received.reshape(1, devices * slots, -1)


def solution(mesh):
    return jax.shard_map(
        per_device,
        mesh=mesh,
        in_specs=(
            P(None, None, "wall", "span"),
            P(),
            P(),
            P(None, "wall"),
            P("wall"),
            P("wall", "span", None, None),
        ),
        out_specs=P(("span", "wall"), None, None),
        check_vma=False,
    )
```
